128 devices in a mesh: row: 8 (over x, z_hi), col: 16 (over y, z_lo, core).
Axes of the slice: x: 4, y: 4, z: 4 (z_hi: 2, z_lo: 2; z = z_hi * 2 + z_lo), core: 2. Of those that a mesh axis runs over, the one named last changes fastest.
Arguments:
- sigma_anc: bfloat16 [4096, 4096], P('row', 'col')
- panel: bfloat16 [48, 4096, 512], P('col', 'row'), may hold values from -0.25 to 0.25
- structure: int32 [48, 4], P('col'), may hold values from 0 to 7, all different within a row
- d_inv: bfloat16 [48, 512, 512], P('col'), may hold values from -6 to 6
- dq_panel: bfloat16 [48, 4096, 512], P('col', 'row'), may hold values from -0.005859375 to 0.005859375
- dq_diag: bfloat16 [48, 512, 512], P('col'), may hold values from -0.01171875 to 0.01171875
Outputs:
- sigma_panel: bfloat16 [48, 4096, 512], P('col', 'row')
- sigma_diag: float32 [48, 512, 512], P('col', 'row')
- trace_part: float32 [48], P('col')
The draws below stay inside these ranges and needn't reach their ends.
Inputs may be any that keep to these rules, and one draw needn't show every extreme that they name: Each row of structure lists 4 different ancestor blocks.
All inputs are finite; a program needn't handle non-finite values.
Results may differ from the reference program's by a relative error of at most 0.001.
Values may be sent and summed in bfloat16 or wider, within the bound.
A program may use at most 128 MiB of HBM per device.

```python
import jax
import jax.numpy as jnp
from jax import lax

W = 512
NB = 8
K = 4
NS = 48


def draw_sigma_anc(key, part):
    order = NB * W
    key_a = jax.random.fold_in(key, 11)
    raw = jax.random.normal(key_a, (order, order), jnp.float32)
    sym = (raw + raw.T) * 0.35355339
    return (sym + jnp.eye(order, dtype=jnp.float32)).astype(jnp.bfloat16)


def block_levels(own_key, dims, shards, smallest, top_value):
    level = 1.0
    for dim, blocks in shards:
        steps = jax.random.uniform(jax.random.fold_in(jax.random.fold_in(own_key, 6), dim), (blocks,), jnp.float32, smallest / len(shards), top_value / len(shards))
        level = level * jnp.repeat(jnp.exp(steps), dims[dim] // blocks).reshape((-1,) + (1,) * (len(dims) - 1 - dim))
    return level


def picks_of(rng, rows, count, top, lift):
    ranking = jax.random.permutation(jax.random.fold_in(rng, 1), count)
    favour = ranking
    for power in range(3):
        favour = favour * favour // count
    favour = favour * lift // count
    chance = jax.random.randint(jax.random.fold_in(rng, 2), (rows, count), 0, 4096) + favour
    fixed_rows = jax.random.permutation(jax.random.fold_in(rng, 3), rows)[jnp.arange(count) % rows]
    chance = jnp.where(jnp.arange(rows)[:, None] == fixed_rows[None, :], 1 << 14, chance)
    priority = chance * count + jnp.arange(count)
    return lax.top_k(priority.astype(jnp.int32), top)[1].astype(jnp.int32)


def scatter_about(rng, extent, scale, most, pieces=(), kind=jnp.bfloat16):
    loudness = block_levels(rng, extent, pieces, -0.22, 0.18) if pieces else 1.0
    result = jax.random.normal(rng, extent, jnp.float32) * scale * loudness
    return jnp.minimum(jnp.maximum(result, -most), most).astype(kind)


def setup_inputs(seed: int = 0) -> dict:
    keys = jax.random.split(jax.random.key(seed), 7)
    sigma_anc = draw_sigma_anc(jax.random.fold_in(keys[6], 71), 0)
    panel = scatter_about(keys[1], (NS, NB * W, W), (K * W // 4) ** -0.5, 0.25, ((0, 16), (1, 8)))
    structure = picks_of(keys[2], NS, NB, K, 0)
    d_inv = scatter_about(keys[3], (NS, W, W), 1.0, 6.0, ((0, 16),))
    dq_panel = scatter_about(keys[4], (NS, NB * W, W), (K * W * W) ** -0.5, 0.005859375, ((0, 16), (1, 8)))
    dq_diag = scatter_about(keys[5], (NS, W, W), (W * W) ** -0.5, 0.01171875, ((0, 16),))
    return dict(sigma_anc=sigma_anc, panel=panel, structure=structure, d_inv=d_inv, dq_panel=dq_panel, dq_diag=dq_diag)


def reference(sigma_anc, panel, structure, d_inv, dq_panel, dq_diag):
    maximum_level = lax.Precision.HIGHEST
    blocks = sigma_anc.reshape(NB, W, NB, W)

    def one_node(items):
        node_panel, node_struct, node_dinv, node_dqp, node_dqd = items
        panel_blocks = node_panel.reshape(NB, W, W)
        dq_blocks = node_dqp.reshape(NB, W, W)
        chosen = blocks[node_struct][:, :, node_struct]
        upper = panel_blocks[node_struct].astype(jnp.float32)
        matrix_product = jnp.einsum("awbv,bvx->awx", chosen.astype(jnp.float32), upper, precision=maximum_level)
        inner_block = jnp.einsum("awx,awy->xy", upper, matrix_product, precision=maximum_level)
        diag = node_dinv.astype(jnp.float32) + inner_block
        trace = -2.0 * jnp.sum(matrix_product * dq_blocks[node_struct].astype(jnp.float32))
        trace = trace + jnp.sum(diag * node_dqd.astype(jnp.float32))
        full = jnp.zeros((NB, W, W), jnp.float32).at[node_struct].set(-matrix_product)
        return full.reshape(NB * W, W).astype(jnp.bfloat16), diag, trace

    sigma_panel, sigma_diag, trace_part = lax.map(one_node, (panel, structure, d_inv, dq_panel, dq_diag))
    return sigma_panel, sigma_diag, trace_part
```

```python
import jax
import jax.numpy as jnp
from jax import lax
from jax.experimental import pallas as pl
from jax.experimental.pallas import tpu as pltpu
from jax.sharding import PartitionSpec as P

MESH = pl.DeviceIdType.MESH
PANEL, DQ, SEL = 0, 1, 2


class Slots:
    def __init__(self):
        self.at = {}

    def __call__(self, *name, span=1):
        if name not in self.at:
            self.at[name] = sum(self.size.values()) if hasattr(self, "size") else 0
            self.size = getattr(self, "size", {})
            self.size[name] = span
        return self.at[name]


def all_slots(ns):
    send, recv = Slots(), Slots()
    for s in (send, recv):
        s("st")
        s("az_own")
        s("az_nb", span=2)
        for d in range(2):
            s("az", d)
            s("az_h", d)
            for j in range(2):
                s("ay", d, j)
                s("ayf", d, j)
            for i in range(ns):
                s("xo", d, i)
                s("xf", d, i)
                for kind in range(3):
                    s("sw", kind, i, d)
        for i in range(ns):
            for part in ("own", "m", "p", "d"):
                s("xs", part, i)
            s("rs1", i)
            for d in range(1, 4):
                s("rs2", i, d)
            s("rs3", i)
        for d in range(1, 8):
            s("tr", d)
    return send, recv, sum(send.size.values())


def kernel(
    struct, sigma, panel, dq, dinv, dqd,
    out_panel, out_diag, out_tr,
    sig, b0, b1, b2, dqv, rb, cbuf, prod, ip, rk, sx, rr, fsrc, fin, dinv_v, dqd_v, trs, tra, st_v, st_s,
    send_sem, recv_sem, loc_sem,
):
    bs = (b0, b1, b2)
    ns = len(bs)
    w = prod.shape[0]
    hw = w // 2
    share = w // 8
    send_at, recv_at, _ = all_slots(ns)

    row, col = lax.axis_index("row"), lax.axis_index("col")
    x, zh = row // 2, row % 2
    y, zl, c = col // 4, (col // 2) % 2, col % 2
    z = zh * 2 + zl
    home = c == zh
    hb = 1 - (c + zh) % 2
    nbp = (hb + zl) % 2
    r = 2 * x + c
    xp, xm, xq = (x + 1) % 4, (x + 3) % 4, (x + 2) % 4
    yp, ym, yq = (y + 1) % 4, (y + 3) % 4, (y + 2) % 4
    zp, zm, zq = (z + 1) % 4, (z + 3) % 4, (z + 2) % 4

    def dev(x_, y_, z_, c_):
        return (x_ * 2 + z_ // 2, (y_ * 2 + z_ % 2) * 2 + c_)

    sib = dev(x, y, z, 1 - c)
    partner = dev(x, y, zq, 1 - c)

    sent = []

    def remote(src, dst, sname, rname, to, soff=0, roff=0):
        return pltpu.make_async_remote_copy(
            src_ref=src,
            dst_ref=dst,
            send_sem=send_sem.at[send_at(*sname) + soff],
            recv_sem=recv_sem.at[recv_at(*rname) + roff],
            device_id=to,
            device_id_type=MESH,
        )

    def go(role, make):
        make().start()
        sent.append((role, make))

    def got(dst, *name, off=0):
        pltpu.make_async_copy(dst, dst, recv_sem.at[recv_at(*name) + off]).wait()

    def local(i, src, dst):
        return pltpu.make_async_copy(src, dst, loc_sem.at[i])

    def at_home(f):
        pl.when(home)(f)

    def at_away(f):
        pl.when(jnp.logical_not(home))(f)

    own_piece = sig.at[4 * y + 2 * zl + c]

    def az_send():
        go("all", lambda: remote(sigma, own_piece, ("az", 0), ("az_nb",), dev(x, y, zp, zh), roff=c))
        go("all", lambda: remote(sigma, own_piece, ("az", 1), ("az_nb",), dev(x, y, zm, zh), roff=c))

    def az_own_away():
        go("away", lambda: remote(sigma, own_piece, ("az_own",), ("az_own",), sib))

    def az_forward():
        for k in range(2):
            got(sig.at[4 * y + 2 * (1 - zl) + k], "az_nb", off=k)
        zd = (z + 1 + 2 * nbp) % 4
        part = sig.at[pl.ds(4 * y + 2 * (1 - zl), 2), pl.ds(pl.multiple_of(nbp * hw, hw), hw)]
        go("all", lambda: pltpu.make_async_remote_copy(
            src_ref=part, dst_ref=part,
            send_sem=send_sem.at[send_at("az_h", 0)],
            recv_sem=recv_sem.at[recv_at("az_h", 0) + nbp * (recv_at("az_h", 1) - recv_at("az_h", 0))],
            device_id=dev(x, y, zd, c), device_id_type=MESH))

    pair_zl = ((zl * hb + (1 - zl) * (1 - hb)), ((1 - zl) * hb + zl * (1 - hb)))

    def pair(y_, j):
        return sig.at[pl.ds(4 * y_ + 2 * pair_zl[j], 2)]

    def ay_send(role, j):
        go(role, lambda: remote(pair(y, j), pair(y, j), ("ay", 0, j), ("ay", 0, j), dev(x, yp, z, c)))
        go(role, lambda: remote(pair(y, j), pair(y, j), ("ay", 1, j), ("ay", 1, j), dev(x, ym, z, c)))

    def ay_forward(j):
        got(pair(ym, j), "ay", 0, j)
        p0 = sig.at[4 * ym + 2 * pair_zl[j]]
        go("all", lambda: remote(p0, p0, ("ayf", 0, j), ("ayf", 0, j), dev(x, yp, z, c)))
        got(pair(yp, j), "ay", 1, j)
        p1 = sig.at[4 * yp + 2 * pair_zl[j] + 1]
        go("all", lambda: remote(p1, p1, ("ayf", 1, j), ("ayf", 1, j), dev(x, ym, z, c)))

    def ay_done():
        for j in range(2):
            for d in range(2):
                got(sig.at[4 * yq + 2 * pair_zl[j] + d], "ayf", d, j)

    def blk(i, x_, c_=None):
        return bs[i].at[2 * x_ + (c if c_ is None else c_)]

    def half(i, x_, d):
        return bs[i].at[2 * x_ + c, pl.ds(d * hw, hw)]

    def to_sib(role, i, part, x_):
        go(role, lambda: remote(blk(i, x_), blk(i, x_), ("xs", part, i), ("xs", part, i), sib))

    def x_own(role, i):
        go(role, lambda: remote(blk(i, x), blk(i, x), ("xo", 0, i), ("xo", 0, i), dev(xp, y, z, c)))
        go(role, lambda: remote(blk(i, x), blk(i, x), ("xo", 1, i), ("xo", 1, i), dev(xm, y, z, c)))
        to_sib(role, i, "own", x)

    def x_forward(role, i):
        got(blk(i, xm), "xo", 0, i)
        go(role, lambda: remote(half(i, xm, 0), half(i, xm, 0), ("xf", 0, i), ("xf", 0, i), dev(xp, y, z, c)))
        got(blk(i, xp), "xo", 1, i)
        go(role, lambda: remote(half(i, xp, 1), half(i, xp, 1), ("xf", 1, i), ("xf", 1, i), dev(xm, y, z, c)))
        to_sib(role, i, "m", xm)
        to_sib(role, i, "p", xp)

    def x_far(role, i):
        for d in range(2):
            got(half(i, xq, d), "xf", d, i)
        to_sib(role, i, "d", xq)

    def x_sib(i):
        for part, x_ in (("own", x), ("m", xm), ("p", xp), ("d", xq)):
            got(blk(i, x_, 1 - c), "xs", part, i)

    ends = (zp, zm)

    def sw_src(kind, i, d):
        rows = pl.ds(d * hw, hw)
        return (panel, dq, cbuf)[kind].at[i, rows]

    def sw_dst(kind, i, d):
        rows = pl.ds(d * hw, hw)
        if kind == PANEL:
            return bs[i].at[2 * x + 1 - ends[d] // 2, rows]
        return (dqv if kind == DQ else out_panel).at[i, rows]

    def sw_send(kind, i):
        for d in range(2):
            go("away", lambda d=d: remote(
                sw_src(kind, i, d), rb.at[3 * kind + i, d], ("sw", kind, i, d), ("sw", kind, i, d),
                dev(x, y, ends[d], ends[d] // 2)))

    def sw_relay(kind, i):
        for d in range(2):
            got(rb.at[3 * kind + i, d], "sw", kind, i, d)
            go("home", lambda d=d: remote(
                rb.at[3 * kind + i, d], sw_dst(kind, i, d), ("sw", kind, i, d), ("sw", kind, i, d),
                dev(x, y, ends[d], 1 - ends[d] // 2)))

    def sw_got(kind, i):
        for d in range(2):
            rows = pl.ds(d * hw, hw)
            dst = bs[i].at[r, rows] if kind == PANEL else (dqv if kind == DQ else out_panel).at[i, rows]
            got(dst, "sw", kind, i, d)

    def compute(i):
        b = bs[i]

        def step(t, carry):
            k = st_s[i, t]
            v = jnp.dot(sig[2 * k], b[k, :hw], preferred_element_type=jnp.float32)
            v += jnp.dot(sig[2 * k + 1], b[k, hw:], preferred_element_type=jnp.float32)
            prod[...] += v
            return carry

        prod[...] = jnp.zeros_like(prod)
        lax.fori_loop(0, 4, step, 0)
        here = jnp.float32(0)
        for t in range(4):
            here += jnp.where(st_s[i, t] == r, jnp.float32(1), jnp.float32(0))
        kept = prod[...] * here
        hi = kept.astype(jnp.bfloat16)
        cbuf[i] = -hi

        def selected_home():
            local(10 + i, cbuf.at[i], out_panel.at[i]).start()

        at_home(selected_home)
        at_away(lambda: sw_send(SEL, i))
        lo = (kept - hi.astype(jnp.float32)).astype(jnp.bfloat16)
        own = b[r]
        inner = lax.dot_general(own, hi, (((0,), (0,)), ((), ())), preferred_element_type=jnp.float32)
        inner += lax.dot_general(own, lo, (((0,), (0,)), ((), ())), preferred_element_type=jnp.float32)
        for a in range(8):
            ip[i, a % 2, a // 2] = inner[a * share : (a + 1) * share]
        go("all", lambda: remote(ip.at[i, 1 - c], rk.at[i], ("rs1", i), ("rs1", i), sib))
        fsrc[i, share:, :] = jnp.zeros((8, w), jnp.float32)
        fsrc[i, share : share + 1, :] = -2.0 * jnp.sum(
            kept * dqv[i].astype(jnp.float32), axis=0, keepdims=True)

    def rs2(i):
        got(rk.at[i], "rs1", i)
        sx[i] = ip[i, c] + rk[i]
        for d in range(1, 4):
            go("all", lambda d=d: remote(
                sx.at[i, (x + d) % 4], rr.at[i, d - 1], ("rs2", i, d), ("rs2", i, d), dev((x + d) % 4, y, z, c)))

    def rs3(i):
        for d in range(1, 4):
            got(rr.at[i, d - 1], "rs2", i, d)
        fsrc[i, :share, :] = sx[i, x] + rr[i, 0] + rr[i, 1] + rr[i, 2]

        def here():
            local(13 + i, fsrc.at[i], fin.at[i]).start()

        at_home(here)
        at_away(lambda: go("away", lambda: remote(fsrc.at[i], fin.at[i], ("rs3", i), ("rs3", i), partner)))

    def finish(i):
        at_home(lambda: local(13 + i, fsrc.at[i], fin.at[i]).wait())
        at_away(lambda: got(fin.at[i], "rs3", i))
        diag = dinv_v[i].astype(jnp.float32) + fin[i, :share]
        out_diag[i] = diag
        part = jnp.sum(diag * dqd_v[i].astype(jnp.float32), axis=0, keepdims=True) + fin[i, share : share + 1]
        part = jnp.sum(part, axis=1, keepdims=True)
        trs[i : i + 1, :] = jnp.broadcast_to(part, (1, 128))

    barrier = pltpu.get_barrier_semaphore()
    peers = [sib, partner, dev(x, yp, z, c), dev(x, ym, z, c)]
    peers += [dev(x, y, z_, c_) for z_ in (zp, zm) for c_ in (0, 1)]
    peers += [((row + d) % 8, col) for d in range(1, 8)]
    for peer in peers:
        pl.semaphore_signal(barrier, inc=1, device_id=peer, device_id_type=MESH)

    my_rows = pl.ds(pl.multiple_of(row * share, share), share)
    at_home(lambda: local(0, struct, st_v).start())
    at_home(lambda: [local(1 + i, panel.at[i], bs[i].at[r]).start() for i in range(ns)] and None)
    at_home(lambda: local(4, sigma, own_piece).start())
    pl.semaphore_wait(barrier, len(peers))

    at_away(lambda: sw_send(PANEL, 0))
    at_home(lambda: go("home", lambda: remote(struct, st_v, ("st",), ("st",), sib)))
    at_away(az_own_away)
    az_send()
    local(5, dinv.at[:, my_rows], dinv_v).start()
    local(6, dqd.at[:, my_rows], dqd_v).start()

    def home_start():
        local(1, panel.at[0], bs[0].at[r]).wait()
        x_own("home", 0)
        local(2, panel.at[1], bs[1].at[r]).wait()
        x_own("home", 1)
        local(4, sigma, own_piece).wait()
        got(sig.at[4 * y + 2 * zl + 1 - c], "az_own")
        ay_send("home", 0)
        local(7, dq, dqv).start()

    def away_start():
        for i in range(1, ns):
            sw_send(PANEL, i)

    at_home(home_start)
    at_away(away_start)
    az_forward()
    at_home(lambda: ay_send("home", 1))
    at_away(lambda: ay_send("away", 0))

    def home_1():
        sw_relay(PANEL, 0)
        x_forward("home", 0)
        local(3, panel.at[2], bs[2].at[r]).wait()
        x_own("home", 2)
        sw_relay(PANEL, 1)

    def away_1():
        sw_got(PANEL, 0)
        x_own("away", 0)
        for d in range(2):
            part = sig.at[pl.ds(4 * y + 2 * zl, 2), pl.ds(d * hw, hw)]
            got(part, "az_h", d)
        ay_send("away", 1)
        sw_got(PANEL, 1)
        x_own("away", 1)

    at_home(home_1)
    at_away(away_1)
    at_home(lambda: sw_relay(PANEL, 2))
    ay_forward(0)

    def away_2():
        sw_got(PANEL, 2)
        x_own("away", 2)
        for i in range(ns):
            sw_send(DQ, i)
        x_forward("away", 0)

    at_home(lambda: x_forward("home", 1))
    at_away(away_2)
    ay_forward(1)

    def home_3():
        x_far("home", 0)
        x_forward("home", 2)
        x_far("home", 1)
        for i in range(ns):
            sw_relay(DQ, i)
        local(0, struct, st_v).wait()
        local(7, dq, dqv).wait()

    def away_3():
        x_forward("away", 1)
        x_far("away", 0)
        x_forward("away", 2)
        x_far("away", 1)
        got(st_v, "st")

    at_home(home_3)
    at_away(away_3)
    cp = local(8, st_v, st_s)
    cp.start()
    cp.wait()
    ay_done()
    x_sib(0)
    at_away(lambda: [sw_got(DQ, i) for i in range(ns)] and None)
    compute(0)
    x_sib(1)
    compute(1)
    rs2(0)
    x_far("all", 2)
    at_home(lambda: sw_relay(SEL, 0))
    rs2(1)
    at_home(lambda: sw_relay(SEL, 1))
    x_sib(2)
    compute(2)
    rs3(0)
    rs3(1)
    rs2(2)
    at_home(lambda: sw_relay(SEL, 2))
    local(5, dinv.at[:, my_rows], dinv_v).wait()
    local(6, dqd.at[:, my_rows], dqd_v).wait()
    trs[...] = jnp.zeros_like(trs)
    finish(0)
    finish(1)
    rs3(2)
    finish(2)
    for d in range(1, 8):
        go("all", lambda d=d: remote(trs, tra.at[d - 1], ("tr", d), ("tr", d), ((row + d) % 8, col)))
    total = trs[...]
    for d in range(1, 8):
        got(tra.at[d - 1], "tr", d)
        total += tra[d - 1]
    out_tr[...] = total

    def home_end():
        for i in range(ns):
            local(10 + i, cbuf.at[i], out_panel.at[i]).wait()
        for role, make in sent:
            if role == "home":
                make().wait_send()

    def away_end():
        for i in range(ns):
            sw_got(SEL, i)
        for role, make in sent:
            if role == "away":
                make().wait_send()

    for role, make in sent:
        if role == "all":
            make().wait_send()
    at_home(home_end)
    at_away(away_end)


def local(sigma_anc, panel, structure, d_inv, dq_panel, dq_diag):
    ns, w = panel.shape[0], panel.shape[2]
    share = w // 8
    slots = all_slots(ns)[2]
    struct = jnp.pad(structure, ((0, 8 - ns), (0, 128 - structure.shape[1])))
    bf, f32 = jnp.bfloat16, jnp.float32
    hbm = pl.BlockSpec(memory_space=pl.ANY)
    vmem = pl.BlockSpec(memory_space=pltpu.VMEM)
    sigma_panel, sigma_diag, tr = pl.pallas_call(
        kernel,
        out_shape=(
            jax.ShapeDtypeStruct((ns, w, w), bf),
            jax.ShapeDtypeStruct((ns, share, w), f32),
            jax.ShapeDtypeStruct((8, 128), f32),
        ),
        in_specs=[hbm] * 6,
        out_specs=(hbm, vmem, vmem),
        scratch_shapes=[
            pltpu.VMEM((16, w, w // 2), bf),
            *[pltpu.VMEM((8, w, w), bf) for _ in range(ns)],
            pltpu.VMEM((ns, w, w), bf),
            pltpu.VMEM((3 * ns, 2, w // 2, w), bf),
            pltpu.VMEM((ns, w, w), bf),
            pltpu.VMEM((w, w), f32),
            pltpu.VMEM((ns, 2, 4, share, w), f32),
            pltpu.VMEM((ns, 4, share, w), f32),
            pltpu.VMEM((ns, 4, share, w), f32),
            pltpu.VMEM((ns, 3, share, w), f32),
            pltpu.VMEM((ns, share + 8, w), f32),
            pltpu.VMEM((ns, share + 8, w), f32),
            pltpu.VMEM((ns, share, w), bf),
            pltpu.VMEM((ns, share, w), bf),
            pltpu.VMEM((8, 128), f32),
            pltpu.VMEM((7, 8, 128), f32),
            pltpu.VMEM((8, 128), jnp.int32),
            pltpu.SMEM((8, 128), jnp.int32),
            pltpu.SemaphoreType.DMA((slots,)),
            pltpu.SemaphoreType.DMA((slots,)),
            pltpu.SemaphoreType.DMA((16,)),
        ],
        compiler_params=pltpu.CompilerParams(
            collective_id=0, has_side_effects=True, vmem_limit_bytes=60 * 1024 * 1024
        ),
        name="selected_inverse",
    )(struct, sigma_anc, panel, dq_panel, d_inv, dq_diag)
    return sigma_panel, sigma_diag, tr[:ns, 0]


def solution(mesh):
    return jax.shard_map(
        local,
        mesh=mesh,
        in_specs=(
            P("row", "col"),
            P("col", "row", None),
            P("col", None),
            P("col", None, None),
            P("col", "row", None),
            P("col", None, None),
        ),
        out_specs=(P("col", "row", None), P("col", "row", None), P("col")),
        check_vma=False,
    )
```

```python
import jax
import jax.numpy as jnp
from jax import lax
from jax.experimental import pallas as pl
from jax.experimental.pallas import tpu as pltpu
from jax.sharding import PartitionSpec as P

MESH = pl.DeviceIdType.MESH
PANEL, DQ, SEL = 0, 1, 2


class Slots:
    def __init__(self):
        self.at = {}

    def __call__(self, *name, span=1):
        if name not in self.at:
            self.at[name] = sum(self.size.values()) if hasattr(self, "size") else 0
            self.size = getattr(self, "size", {})
            self.size[name] = span
        return self.at[name]


def all_slots(ns):
    send, recv = Slots(), Slots()
    for s in (send, recv):
        s("st")
        s("az_own")
        s("az_nb", span=2)
        for d in range(2):
            s("az", d)
            s("az_h", d)
            for j in range(2):
                s("ay", d, j)
                s("ayf", d, j)
            for i in range(ns):
                s("xo", d, i)
                s("xf", d, i)
                for kind in range(3):
                    s("sw", kind, i, d)
        for i in range(ns):
            for part in ("own", "m", "p", "d"):
                s("xs", part, i)
            s("rs1", i)
            for d in range(2):
                s("rsa", i, d)
                s("rsb", i, d)
            s("rs3", i)
        s("dqd")
        s("tr", span=8)
    return send, recv, sum(send.size.values())


def kernel(
    struct, sigma, panel, dq, dinv, dqd,
    out_panel, out_diag, out_tr,
    sig, b0, b1, b2, dqv, rb, cbuf, prod, ip, rk, sx, ra, rr, fsrc, fin, dinv_v, dqd_all, dqd_v, tp, td, trs, tra,
    st_v, st_s,
    send_sem, recv_sem, loc_sem,
):
    bs = (b0, b1, b2)
    ns = len(bs)
    w = prod.shape[0]
    hw = w // 2
    share = w // 8
    send_at, recv_at, _ = all_slots(ns)

    row, col = lax.axis_index("row"), lax.axis_index("col")
    x, zh = row // 2, row % 2
    y, zl, c = col // 4, (col // 2) % 2, col % 2
    z = zh * 2 + zl
    home = c == zh
    hb = 1 - (c + zh) % 2
    nbp = (hb + zl) % 2
    r = 2 * x + c
    xp, xm, xq = (x + 1) % 4, (x + 3) % 4, (x + 2) % 4
    yp, ym, yq = (y + 1) % 4, (y + 3) % 4, (y + 2) % 4
    zp, zm, zq = (z + 1) % 4, (z + 3) % 4, (z + 2) % 4

    def dev(x_, y_, z_, c_):
        return (x_ * 2 + z_ // 2, (y_ * 2 + z_ % 2) * 2 + c_)

    sib = dev(x, y, z, 1 - c)
    partner = dev(x, y, zq, 1 - c)

    sent = []

    def remote(src, dst, sname, rname, to, soff=0, roff=0):
        return pltpu.make_async_remote_copy(
            src_ref=src,
            dst_ref=dst,
            send_sem=send_sem.at[send_at(*sname) + soff],
            recv_sem=recv_sem.at[recv_at(*rname) + roff],
            device_id=to,
            device_id_type=MESH,
        )

    def go(role, make):
        make().start()
        sent.append((role, make))

    def got(dst, *name, off=0):
        pltpu.make_async_copy(dst, dst, recv_sem.at[recv_at(*name) + off]).wait()

    def local(i, src, dst):
        return pltpu.make_async_copy(src, dst, loc_sem.at[i])

    def at_home(f):
        pl.when(home)(f)

    def at_away(f):
        pl.when(jnp.logical_not(home))(f)

    own_piece = sig.at[4 * y + 2 * zl + c]

    def az_send():
        go("all", lambda: remote(sigma, own_piece, ("az", 0), ("az_nb",), dev(x, y, zp, zh), roff=c))
        go("all", lambda: remote(sigma, own_piece, ("az", 1), ("az_nb",), dev(x, y, zm, zh), roff=c))

    def az_own_away():
        go("away", lambda: remote(sigma, own_piece, ("az_own",), ("az_own",), sib))

    def az_forward():
        for k in range(2):
            got(sig.at[4 * y + 2 * (1 - zl) + k], "az_nb", off=k)
        zd = (z + 1 + 2 * nbp) % 4
        part = sig.at[pl.ds(4 * y + 2 * (1 - zl), 2), pl.ds(pl.multiple_of(nbp * hw, hw), hw)]
        go("all", lambda: pltpu.make_async_remote_copy(
            src_ref=part, dst_ref=part,
            send_sem=send_sem.at[send_at("az_h", 0)],
            recv_sem=recv_sem.at[recv_at("az_h", 0) + nbp * (recv_at("az_h", 1) - recv_at("az_h", 0))],
            device_id=dev(x, y, zd, c), device_id_type=MESH))

    pair_zl = ((zl * hb + (1 - zl) * (1 - hb)), ((1 - zl) * hb + zl * (1 - hb)))

    def pair(y_, j):
        return sig.at[pl.ds(4 * y_ + 2 * pair_zl[j], 2)]

    def ay_send(role, j):
        go(role, lambda: remote(pair(y, j), pair(y, j), ("ay", 0, j), ("ay", 0, j), dev(x, yp, z, c)))
        go(role, lambda: remote(pair(y, j), pair(y, j), ("ay", 1, j), ("ay", 1, j), dev(x, ym, z, c)))

    def ay_forward(j):
        got(pair(ym, j), "ay", 0, j)
        p0 = sig.at[4 * ym + 2 * pair_zl[j]]
        go("all", lambda: remote(p0, p0, ("ayf", 0, j), ("ayf", 0, j), dev(x, yp, z, c)))
        got(pair(yp, j), "ay", 1, j)
        p1 = sig.at[4 * yp + 2 * pair_zl[j] + 1]
        go("all", lambda: remote(p1, p1, ("ayf", 1, j), ("ayf", 1, j), dev(x, ym, z, c)))

    def ay_done():
        for j in range(2):
            for d in range(2):
                got(sig.at[4 * yq + 2 * pair_zl[j] + d], "ayf", d, j)

    def blk(i, x_, c_=None):
        return bs[i].at[2 * x_ + (c if c_ is None else c_)]

    def half(i, x_, d):
        return bs[i].at[2 * x_ + c, pl.ds(d * hw, hw)]

    def to_sib(role, i, part, x_):
        go(role, lambda: remote(blk(i, x_), blk(i, x_), ("xs", part, i), ("xs", part, i), sib))

    def x_own(role, i):
        go(role, lambda: remote(blk(i, x), blk(i, x), ("xo", 0, i), ("xo", 0, i), dev(xp, y, z, c)))
        go(role, lambda: remote(blk(i, x), blk(i, x), ("xo", 1, i), ("xo", 1, i), dev(xm, y, z, c)))
        to_sib(role, i, "own", x)

    def x_forward(role, i):
        got(blk(i, xm), "xo", 0, i)
        go(role, lambda: remote(half(i, xm, 0), half(i, xm, 0), ("xf", 0, i), ("xf", 0, i), dev(xp, y, z, c)))
        got(blk(i, xp), "xo", 1, i)
        go(role, lambda: remote(half(i, xp, 1), half(i, xp, 1), ("xf", 1, i), ("xf", 1, i), dev(xm, y, z, c)))
        to_sib(role, i, "m", xm)
        to_sib(role, i, "p", xp)

    def x_far(role, i):
        for d in range(2):
            got(half(i, xq, d), "xf", d, i)
        to_sib(role, i, "d", xq)

    def x_sib(i):
        for part, x_ in (("own", x), ("m", xm), ("p", xp), ("d", xq)):
            got(blk(i, x_, 1 - c), "xs", part, i)

    ends = (zp, zm)

    def sw_src(kind, i, d):
        rows = pl.ds(d * hw, hw)
        return (panel, dq, cbuf)[kind].at[i, rows]

    def sw_dst(kind, i, d):
        rows = pl.ds(d * hw, hw)
        if kind == PANEL:
            return bs[i].at[2 * x + 1 - ends[d] // 2, rows]
        return (dqv if kind == DQ else out_panel).at[i, rows]

    def sw_send(kind, i):
        for d in range(2):
            go("away", lambda d=d: remote(
                sw_src(kind, i, d), rb.at[3 * kind + i, d], ("sw", kind, i, d), ("sw", kind, i, d),
                dev(x, y, ends[d], ends[d] // 2)))

    def sw_relay(kind, i):
        for d in range(2):
            got(rb.at[3 * kind + i, d], "sw", kind, i, d)
            go("home", lambda d=d: remote(
                rb.at[3 * kind + i, d], sw_dst(kind, i, d), ("sw", kind, i, d), ("sw", kind, i, d),
                dev(x, y, ends[d], 1 - ends[d] // 2)))

    def sw_got(kind, i):
        for d in range(2):
            rows = pl.ds(d * hw, hw)
            dst = bs[i].at[r, rows] if kind == PANEL else (dqv if kind == DQ else out_panel).at[i, rows]
            got(dst, "sw", kind, i, d)

    def compute(i):
        b = bs[i]

        def step(t, carry):
            k = st_s[i, t]
            v = jnp.dot(sig[2 * k], b[k, :hw], preferred_element_type=jnp.float32)
            v += jnp.dot(sig[2 * k + 1], b[k, hw:], preferred_element_type=jnp.float32)
            prod[...] += v
            return carry

        prod[...] = jnp.zeros_like(prod)
        lax.fori_loop(0, 4, step, 0)
        here = jnp.float32(0)
        for t in range(4):
            here += jnp.where(st_s[i, t] == r, jnp.float32(1), jnp.float32(0))
        kept = prod[...] * here
        hi = kept.astype(jnp.bfloat16)
        cbuf[i] = -hi

        def selected_home():
            local(10 + i, cbuf.at[i], out_panel.at[i]).start()

        at_home(selected_home)
        at_away(lambda: sw_send(SEL, i))
        lo = (kept - hi.astype(jnp.float32)).astype(jnp.bfloat16)
        own = b[r]
        inner = lax.dot_general(own, hi, (((0,), (0,)), ((), ())), preferred_element_type=jnp.float32)
        inner += lax.dot_general(own, lo, (((0,), (0,)), ((), ())), preferred_element_type=jnp.float32)
        for a in range(8):
            ip[i, a % 2, a // 2] = inner[a * share : (a + 1) * share]
        go("all", lambda: remote(ip.at[i, 1 - c], rk.at[i], ("rs1", i), ("rs1", i), sib))
        tp[i : i + 1, :] = -2.0 * jnp.sum(kept * dqv[i].astype(jnp.float32), axis=0, keepdims=True)

    hs = share // 2
    near = (xp, xm)

    def rs_a(i):
        got(rk.at[i], "rs1", i)
        sx[i] = ip[i, c] + rk[i]
        for d in range(2):
            go("all", lambda d=d: remote(
                sx.at[i, xq, pl.ds(d * hs, hs)], ra.at[i, d], ("rsa", i, d), ("rsa", i, d), dev(near[d], y, z, c)))

    def rs_b(i):
        for d in range(2):
            got(ra.at[i, d], "rsa", i, d)
            sx[i, near[d], d * hs : (d + 1) * hs, :] += ra[i, d]
            go("all", lambda d=d: remote(
                sx.at[i, near[d]], rr.at[i, d], ("rsb", i, d), ("rsb", i, d), dev(near[d], y, z, c)))

    def rs_c(i):
        for d in range(2):
            got(rr.at[i, d], "rsb", i, d)
        total = sx[i, x] + rr[i, 0] + rr[i, 1]
        fsrc[i] = total

        def here():
            local(13 + i, fsrc.at[i], fin.at[i]).start()

        at_home(here)
        at_away(lambda: go("away", lambda: remote(fsrc.at[i], fin.at[i], ("rs3", i), ("rs3", i), partner)))
        part = jnp.sum(total * dqd_v[i].astype(jnp.float32), axis=0, keepdims=True) + tp[i : i + 1, :]
        trs[i : i + 1, :] = jnp.broadcast_to(jnp.sum(part, axis=1, keepdims=True), (1, 128))

    def finish(i):
        at_home(lambda: local(13 + i, fsrc.at[i], fin.at[i]).wait())
        at_away(lambda: got(fin.at[i], "rs3", i))
        out_diag[i] = dinv_v[i, my_rows].astype(jnp.float32) + fin[i]

    def trace_send():
        for dx in range(4):
            for dz in range(2):
                to = dev((x + dx) % 4, y, (z + 2 * dz) % 4, zh)

                def make(dx=dx, dz=dz, to=to):
                    return pltpu.make_async_remote_copy(
                        src_ref=trs, dst_ref=tra.at[2 * dx + c],
                        send_sem=send_sem.at[send_at("tr") + 2 * dx + dz],
                        recv_sem=recv_sem.at[recv_at("tr") + 2 * dx + c],
                        device_id=to, device_id_type=MESH)

                if dx == 0 and dz == 0:
                    def mine():
                        tra[c] = trs[...]

                    at_home(mine)
                    at_away(lambda make=make: go("away", make))
                else:
                    go("all", make)

    def trace_got():
        at_home(lambda: got(tra.at[1 - c], "tr", off=1 - c))

        def both():
            for k in range(2):
                got(tra.at[k], "tr", off=k)

        at_away(both)
        total = tra[0] + tra[1]
        for k in range(2, 8):
            got(tra.at[k], "tr", off=k)
            total += tra[k]
        out_tr[...] = total + td[...]

    def own_trace():
        local(5, dinv, dinv_v).wait()
        local(6, dqd, dqd_all).wait()
        td[...] = jnp.zeros_like(td)
        for i in range(ns):
            v = jnp.sum(dinv_v[i].astype(jnp.float32) * dqd_all[i].astype(jnp.float32), axis=0, keepdims=True)
            td[i : i + 1, :] = jnp.broadcast_to(jnp.sum(v, axis=1, keepdims=True), (1, 128))

    barrier = pltpu.get_barrier_semaphore()
    peers = [dev(x, yp, z, c), dev(x, ym, z, c)]
    peers += [dev(x, y, z_, c_) for z_ in (zp, zm) for c_ in (0, 1)]
    for x_ in (x, xp, xm, xq):
        for z_ in (z, zq):
            for c_ in (c, 1 - c):
                if not (x_ is x and z_ is z and c_ is c):
                    peers.append(dev(x_, y, z_, c_))
    for peer in peers:
        pl.semaphore_signal(barrier, inc=1, device_id=peer, device_id_type=MESH)

    my_rows = pl.ds(pl.multiple_of(row * share, share), share)
    at_home(lambda: [local(1 + i, panel.at[i], bs[i].at[r]).start() for i in range(ns)] and None)
    at_home(lambda: local(4, sigma, own_piece).start())

    def structure_out():
        rows = lax.broadcasted_iota(jnp.int32, st_v.shape, 0)
        cols = lax.broadcasted_iota(jnp.int32, st_v.shape, 1)
        v = jnp.zeros(st_v.shape, jnp.int32)
        for i in range(ns):
            for t in range(4):
                v = jnp.where((rows == i) & (cols == t), struct[i, t], v)
        st_v[...] = v

    at_home(structure_out)
    pl.semaphore_wait(barrier, len(peers))

    az_send()
    at_away(az_own_away)
    at_away(lambda: sw_send(PANEL, 0))
    at_home(lambda: go("home", lambda: remote(st_v, st_v, ("st",), ("st",), sib)))
    local(5, dinv, dinv_v).start()
    local(6, dqd, dqd_all).start()

    def home_start():
        local(1, panel.at[0], bs[0].at[r]).wait()
        x_own("home", 0)
        local(2, panel.at[1], bs[1].at[r]).wait()
        x_own("home", 1)
        local(4, sigma, own_piece).wait()
        got(sig.at[4 * y + 2 * zl + 1 - c], "az_own")
        ay_send("home", 0)
        local(7, dq, dqv).start()
        local(9, dqd.at[:, my_rows], dqd_v).start()

    def away_start():
        for i in range(1, ns):
            sw_send(PANEL, i)

    at_home(home_start)
    at_away(away_start)
    az_forward()
    at_home(lambda: ay_send("home", 1))
    at_away(lambda: ay_send("away", 0))

    def home_1():
        x_forward("home", 0)
        local(3, panel.at[2], bs[2].at[r]).wait()
        x_own("home", 2)

    def home_2():
        sw_relay(PANEL, 0)
        x_forward("home", 1)
        sw_relay(PANEL, 1)

    def away_1():
        for d in range(2):
            part = sig.at[pl.ds(4 * y + 2 * zl, 2), pl.ds(d * hw, hw)]
            got(part, "az_h", d)
        ay_send("away", 1)
        sw_got(PANEL, 0)
        x_own("away", 0)

    def away_2():
        sw_got(PANEL, 1)
        x_own("away", 1)

    at_home(home_1)
    at_away(away_1)
    ay_forward(0)
    at_home(home_2)
    at_away(away_2)
    ay_forward(1)

    def home_3():
        sw_relay(PANEL, 2)
        x_far("home", 0)
        x_forward("home", 2)
        x_far("home", 1)
        x_far("home", 2)
        for i in range(ns):
            sw_relay(DQ, i)
        local(7, dq, dqv).wait()
        local(9, dqd.at[:, my_rows], dqd_v).wait()

    def away_3():
        sw_got(PANEL, 2)
        x_own("away", 2)
        for i in range(ns):
            sw_send(DQ, i)
        go("away", lambda: remote(dqd.at[:, my_rows], dqd_v, ("dqd",), ("dqd",), partner))
        got(st_v, "st")
        x_forward("away", 0)
        x_forward("away", 1)
        x_far("away", 0)
        sw_got(DQ, 0)

    own_trace()
    at_home(home_3)
    at_away(away_3)
    cp = local(8, st_v, st_s)
    cp.start()
    cp.wait()
    trs[...] = jnp.zeros_like(trs)
    ay_done()
    x_sib(0)
    compute(0)

    def away_4():
        x_forward("away", 2)
        x_far("away", 1)
        sw_got(DQ, 1)

    at_away(away_4)
    rs_a(0)
    x_sib(1)
    compute(1)
    at_home(lambda: sw_relay(SEL, 0))
    rs_b(0)
    rs_a(1)

    def away_5():
        x_far("away", 2)
        sw_got(DQ, 2)

    at_away(away_5)
    x_sib(2)
    compute(2)
    rs_b(1)
    rs_a(2)
    at_home(lambda: sw_relay(SEL, 1))
    at_away(lambda: got(dqd_v, "dqd"))
    rs_c(0)
    rs_c(1)
    rs_b(2)
    at_home(lambda: sw_relay(SEL, 2))
    finish(0)
    finish(1)
    rs_c(2)
    trace_send()
    finish(2)
    trace_got()

    def home_end():
        for i in range(ns):
            local(10 + i, cbuf.at[i], out_panel.at[i]).wait()
        for role, make in sent:
            if role == "home":
                make().wait_send()

    def away_end():
        for i in range(ns):
            sw_got(SEL, i)
        for role, make in sent:
            if role == "away":
                make().wait_send()

    for role, make in sent:
        if role == "all":
            make().wait_send()
    at_home(home_end)
    at_away(away_end)


def local(sigma_anc, panel, structure, d_inv, dq_panel, dq_diag):
    ns, w = panel.shape[0], panel.shape[2]
    share = w // 8
    slots = all_slots(ns)[2]
    bf, f32 = jnp.bfloat16, jnp.float32
    hbm = pl.BlockSpec(memory_space=pl.ANY)
    vmem = pl.BlockSpec(memory_space=pltpu.VMEM)
    sigma_panel, sigma_diag, tr = pl.pallas_call(
        kernel,
        out_shape=(
            jax.ShapeDtypeStruct((ns, w, w), bf),
            jax.ShapeDtypeStruct((ns, share, w), f32),
            jax.ShapeDtypeStruct((8, 128), f32),
        ),
        in_specs=[pl.BlockSpec(memory_space=pltpu.SMEM)] + [hbm] * 5,
        out_specs=(hbm, vmem, vmem),
        scratch_shapes=[
            pltpu.VMEM((16, w, w // 2), bf),
            *[pltpu.VMEM((8, w, w), bf) for _ in range(ns)],
            pltpu.VMEM((ns, w, w), bf),
            pltpu.VMEM((3 * ns, 2, w // 2, w), bf),
            pltpu.VMEM((ns, w, w), bf),
            pltpu.VMEM((w, w), f32),
            pltpu.VMEM((ns, 2, 4, share, w), f32),
            pltpu.VMEM((ns, 4, share, w), f32),
            pltpu.VMEM((ns, 4, share, w), f32),
            pltpu.VMEM((ns, 2, share // 2, w), f32),
            pltpu.VMEM((ns, 2, share, w), f32),
            pltpu.VMEM((ns, share, w), f32),
            pltpu.VMEM((ns, share, w), f32),
            pltpu.VMEM((ns, w, w), bf),
            pltpu.VMEM((ns, w, w), bf),
            pltpu.VMEM((ns, share, w), bf),
            pltpu.VMEM((8, w), f32),
            pltpu.VMEM((8, 128), f32),
            pltpu.VMEM((8, 128), f32),
            pltpu.VMEM((8, 8, 128), f32),
            pltpu.VMEM((8, 128), jnp.int32),
            pltpu.SMEM((8, 128), jnp.int32),
            pltpu.SemaphoreType.DMA((slots,)),
            pltpu.SemaphoreType.DMA((slots,)),
            pltpu.SemaphoreType.DMA((16,)),
        ],
        compiler_params=pltpu.CompilerParams(
            collective_id=0, has_side_effects=True, vmem_limit_bytes=60 * 1024 * 1024
        ),
        name="selected_inverse",
    )(structure, sigma_anc, panel, dq_panel, d_inv, dq_diag)
    return sigma_panel, sigma_diag, tr[:ns, 0]


def solution(mesh):
    return jax.shard_map(
        local,
        mesh=mesh,
        in_specs=(
            P("row", "col"),
            P("col", "row", None),
            P("col", None),
            P("col", None, None),
            P("col", "row", None),
            P("col", None, None),
        ),
        out_specs=(P("col", "row", None), P("col", "row", None), P("col")),
        check_vma=False,
    )
```

```python
import functools

import jax
import jax.numpy as jnp
from jax import lax
from jax.experimental import pallas as pl
from jax.experimental.pallas import tpu as pltpu
from jax.sharding import PartitionSpec as P

MESH = pl.DeviceIdType.MESH
PANEL, DQ, SEL = 0, 1, 2
SPLIT = (2, 1, 2)


def chunks_of(ns, w):
    out = []
    for i in range(ns):
        n = SPLIT[i % len(SPLIT)]
        out += [(i, j * (w // n), w // n) for j in range(n)]
    return out


class Slots:
    def __init__(self):
        self.at = {}

    def __call__(self, *name, span=1):
        if name not in self.at:
            self.at[name] = sum(self.size.values()) if hasattr(self, "size") else 0
            self.size = getattr(self, "size", {})
            self.size[name] = span
        return self.at[name]


def all_slots(ns, nk):
    send, recv = Slots(), Slots()
    for s in (send, recv):
        s("st")
        s("az_own")
        s("az_nb", span=2)
        s("az_far", span=2)
        s("az", 2)
        for d in range(2):
            s("az", d)
            for j in range(2):
                s("ay", d, j)
                s("ayf", d, j)
            for i in range(nk):
                s("xo", d, i)
                s("xf", d, i)
                s("rsa", i, d)
                s("rsb", i, d)
        for i in range(nk):
            for part in ("own", "m", "p", "d"):
                s("xs", part, i)
            s("sw", PANEL, i)
            s("sw", SEL, i)
            s("rs1", i)
            s("rs3", i)
        for i in range(ns):
            s("sw", DQ, i)
        s("dqd")
        s("tr", span=8)
    return send, recv, sum(send.size.values())


def kernel(
    chunks, struct, sigma, panel, dq, dqd, dinv,
    out_panel, out_sum, out_tr,
    sig, *rest,
):
    nk = len(chunks)
    ns = chunks[-1][0] + 1
    bs = rest[:nk]
    (dqv, cbuf, ip, rk, sx, ra, rr, fsrc, dqd_v, dinv_v, own_v, td, trs, st_v, st_s,
     send_sem, recv_sem, loc_sem) = rest[nk + 1 :]
    prod = rest[nk]
    w = dqv.shape[1]
    hw = w // 2
    share = w // 8
    send_at, recv_at, _ = all_slots(ns, nk)

    row, col = lax.axis_index("row"), lax.axis_index("col")
    x, zh = row // 2, row % 2
    y, zl, c = col // 4, (col // 2) % 2, col % 2
    z = zh * 2 + zl
    home = c == zh
    hb = 1 - (c + zh) % 2
    r = 2 * x + c
    xp, xm, xq = (x + 1) % 4, (x + 3) % 4, (x + 2) % 4
    yp, ym, yq = (y + 1) % 4, (y + 3) % 4, (y + 2) % 4
    zp, zm, zq = (z + 1) % 4, (z + 3) % 4, (z + 2) % 4

    def dev(x_, y_, z_, c_):
        return (x_ * 2 + z_ // 2, (y_ * 2 + z_ % 2) * 2 + c_)

    sib = dev(x, y, z, 1 - c)
    partner = dev(x, y, zq, 1 - c)

    sent = []

    def remote(src, dst, sname, rname, to, soff=0, roff=0):
        return pltpu.make_async_remote_copy(
            src_ref=src,
            dst_ref=dst,
            send_sem=send_sem.at[send_at(*sname) + soff],
            recv_sem=recv_sem.at[recv_at(*rname) + roff],
            device_id=to,
            device_id_type=MESH,
        )

    def go(role, make):
        make().start()
        sent.append((role, make))

    def got(dst, *name, off=0):
        pltpu.make_async_copy(dst, dst, recv_sem.at[recv_at(*name) + off]).wait()

    def local(i, src, dst):
        return pltpu.make_async_copy(src, dst, loc_sem.at[i])

    def at_home(f):
        pl.when(home)(f)

    def at_away(f):
        pl.when(jnp.logical_not(home))(f)

    own_piece = sig.at[4 * y + 2 * zl + c]

    def az_send():
        go("all", lambda: remote(sigma, own_piece, ("az", 0), ("az_nb",), dev(x, y, zp, zh), roff=c))
        go("all", lambda: remote(sigma, own_piece, ("az", 1), ("az_nb",), dev(x, y, zm, zh), roff=c))
        go("all", lambda: remote(sigma, own_piece, ("az", 2), ("az_far",), dev(x, y, zq, zh), roff=c))

    def az_own_away():
        go("away", lambda: remote(sigma, own_piece, ("az_own",), ("az_own",), sib))

    def az_near():
        for k in range(2):
            got(sig.at[4 * y + 2 * (1 - zl) + k], "az_nb", off=k)

    def az_far():
        for k in range(2):
            got(sig.at[4 * y + 2 * zl + k], "az_far", off=k)

    pair_zl = ((zl * hb + (1 - zl) * (1 - hb)), ((1 - zl) * hb + zl * (1 - hb)))

    def pair(y_, j):
        return sig.at[pl.ds(4 * y_ + 2 * pair_zl[j], 2)]

    def ay_send(role, j):
        go(role, lambda: remote(pair(y, j), pair(y, j), ("ay", 0, j), ("ay", 0, j), dev(x, yp, z, c)))
        go(role, lambda: remote(pair(y, j), pair(y, j), ("ay", 1, j), ("ay", 1, j), dev(x, ym, z, c)))

    def ay_forward(j):
        got(pair(ym, j), "ay", 0, j)
        p0 = sig.at[4 * ym + 2 * pair_zl[j]]
        go("all", lambda: remote(p0, p0, ("ayf", 0, j), ("ayf", 0, j), dev(x, yp, z, c)))
        got(pair(yp, j), "ay", 1, j)
        p1 = sig.at[4 * yp + 2 * pair_zl[j] + 1]
        go("all", lambda: remote(p1, p1, ("ayf", 1, j), ("ayf", 1, j), dev(x, ym, z, c)))

    def ay_done():
        for j in range(2):
            for d in range(2):
                got(sig.at[4 * yq + 2 * pair_zl[j] + d], "ayf", d, j)

    def blk(i, x_, c_=None):
        return bs[i].at[2 * x_ + (c if c_ is None else c_)]

    def half(i, x_, d):
        return bs[i].at[2 * x_ + c, pl.ds(d * hw, hw)]

    def to_sib(role, i, part, x_):
        go(role, lambda: remote(blk(i, x_), blk(i, x_), ("xs", part, i), ("xs", part, i), sib))

    def x_own(role, i):
        go(role, lambda: remote(blk(i, x), blk(i, x), ("xo", 0, i), ("xo", 0, i), dev(xp, y, z, c)))
        go(role, lambda: remote(blk(i, x), blk(i, x), ("xo", 1, i), ("xo", 1, i), dev(xm, y, z, c)))
        to_sib(role, i, "own", x)

    def x_forward(role, i):
        got(blk(i, xm), "xo", 0, i)
        go(role, lambda: remote(half(i, xm, 0), half(i, xm, 0), ("xf", 0, i), ("xf", 0, i), dev(xp, y, z, c)))
        got(blk(i, xp), "xo", 1, i)
        go(role, lambda: remote(half(i, xp, 1), half(i, xp, 1), ("xf", 1, i), ("xf", 1, i), dev(xm, y, z, c)))
        to_sib(role, i, "m", xm)
        to_sib(role, i, "p", xp)

    def x_far(role, i):
        for d in range(2):
            got(half(i, xq, d), "xf", d, i)
        to_sib(role, i, "d", xq)

    def x_sib(i):
        for part, x_ in (("own", x), ("m", xm), ("p", xp), ("d", xq)):
            got(blk(i, x_, 1 - c), "xs", part, i)

    def cols(i):
        return chunks[i][0], slice(None), pl.ds(chunks[i][1], chunks[i][2])

    def sw_dst(kind, i, r_):
        if kind == PANEL:
            return bs[i].at[r_]
        return dqv.at[i] if kind == DQ else out_panel.at[cols(i)]

    def sw_send(kind, i):
        def make():
            src = panel.at[cols(i)] if kind == PANEL else dq.at[i] if kind == DQ else cbuf.at[cols(i)]
            return remote(src, sw_dst(kind, i, 2 * x + 1 - c), ("sw", kind, i), ("sw", kind, i), partner)

        go("away", make)

    def sw_got(kind, i):
        got(sw_dst(kind, i, r), "sw", kind, i)

    def compute(i):
        b = bs[i]
        s, off, wc = chunks[i]
        lanes = slice(off, off + wc)

        def step(t, carry):
            k = st_s[s, t]
            v = jnp.dot(sig[2 * k], b[k, :hw], preferred_element_type=jnp.float32)
            v += jnp.dot(sig[2 * k + 1], b[k, hw:], preferred_element_type=jnp.float32)
            prod[:, :wc] += v
            return carry

        prod[:, :wc] = jnp.zeros((w, wc), jnp.float32)
        lax.fori_loop(0, 4, step, 0)
        here = jnp.float32(0)
        for t in range(4):
            here += jnp.where(st_s[s, t] == r, jnp.float32(1), jnp.float32(0))
        kept = prod[:, :wc] * here
        hi = kept.astype(jnp.bfloat16)
        cbuf[s, :, lanes] = -hi

        def selected_home():
            local(10 + i, cbuf.at[cols(i)], out_panel.at[cols(i)]).start()

        at_home(selected_home)
        at_away(lambda: sw_send(SEL, i))
        lo = (kept - hi.astype(jnp.float32)).astype(jnp.bfloat16)
        trace = -2.0 * jnp.sum(kept * dqv[s, :, lanes].astype(jnp.float32), axis=0, keepdims=True)
        for i2, (s2, off2, wc2) in enumerate(chunks):
            if s2 != s:
                continue
            own = bs[i2][r]
            inner = lax.dot_general(own, hi, (((0,), (0,)), ((), ())), preferred_element_type=jnp.float32)
            inner += lax.dot_general(own, lo, (((0,), (0,)), ((), ())), preferred_element_type=jnp.float32)
            for a in range(wc2 // share):
                a2 = off2 // share + a
                ip[s, a2 % 2, a2 // 2, :, lanes] = inner[a * share : (a + 1) * share]
            weight = dqd_v[s, off2 : off2 + wc2, lanes].astype(jnp.float32)
            trace += jnp.sum(inner * weight, axis=0, keepdims=True)
        go("all", lambda: remote(
            ip.at[s, 1 - c, :, :, pl.ds(off, wc)], rk.at[s, :, :, pl.ds(off, wc)], ("rs1", i), ("rs1", i), sib))
        trs[s : s + 1, :] += jnp.broadcast_to(jnp.sum(trace, axis=1, keepdims=True), (1, 128))

    hs = share // 2
    near = (xp, xm)

    def rs_a(i):
        s, off, wc = chunks[i]
        lanes, part = slice(off, off + wc), pl.ds(off, wc)
        got(rk.at[s, :, :, part], "rs1", i)
        sx[s, :, :, lanes] = ip[s, c, :, :, lanes] + rk[s, :, :, lanes]
        for d in range(2):
            go("all", lambda d=d: remote(
                sx.at[s, xq, pl.ds(d * hs, hs), part], ra.at[s, d, :, part], ("rsa", i, d), ("rsa", i, d),
                dev(near[d], y, z, c)))

    def rs_b(i):
        s, off, wc = chunks[i]
        lanes, part = slice(off, off + wc), pl.ds(off, wc)
        for d in range(2):
            got(ra.at[s, d, :, part], "rsa", i, d)
            sx[s, near[d], d * hs : (d + 1) * hs, lanes] += ra[s, d, :, lanes]
            go("all", lambda d=d: remote(
                sx.at[s, near[d], :, part], rr.at[s, d, :, part], ("rsb", i, d), ("rsb", i, d),
                dev(near[d], y, z, c)))

    def rs_c(i):
        s, off, wc = chunks[i]
        lanes, part = slice(off, off + wc), pl.ds(off, wc)
        for d in range(2):
            got(rr.at[s, d, :, part], "rsb", i, d)
        total = sx[s, x, :, lanes] + rr[s, 0, :, lanes] + rr[s, 1, :, lanes]
        fsrc[s, :, lanes] = total

        def here():
            local(26 + i, fsrc.at[s, :, part], out_sum.at[s, :, part]).start()

        at_home(here)
        at_away(lambda: go("away", lambda: remote(
            fsrc.at[s, :, part], out_sum.at[s, :, part], ("rs3", i), ("rs3", i), partner)))

    def own_trace():
        local(4, dinv, dinv_v).wait()
        local(5, dqd, own_v).wait()
        td[...] = jnp.zeros_like(td)
        for i in range(ns):
            v = jnp.sum(dinv_v[i].astype(jnp.float32) * own_v[i].astype(jnp.float32), axis=0, keepdims=True)
            td[i : i + 1, :] = jnp.broadcast_to(jnp.sum(v, axis=1, keepdims=True), (1, 128))
        local(6, td, out_tr.at[8]).start()

    def trace_send():
        for dx in range(4):
            for dz in range(2):
                to = dev((x + dx) % 4, y, (z + 2 * dz) % 4, zh)

                def make(dx=dx, dz=dz, to=to):
                    return pltpu.make_async_remote_copy(
                        src_ref=trs, dst_ref=out_tr.at[2 * dx + c],
                        send_sem=send_sem.at[send_at("tr") + 2 * dx + dz],
                        recv_sem=recv_sem.at[recv_at("tr") + 2 * dx + c],
                        device_id=to, device_id_type=MESH)

                if dx == 0 and dz == 0:
                    at_home(lambda: local(8, trs, out_tr.at[c]).start())
                    at_away(lambda make=make: go("away", make))
                else:
                    go("all", make)

    def trace_got():
        local(6, td, out_tr.at[8]).wait()
        def mine():
            got(out_tr.at[1 - c], "tr", off=1 - c)
            local(8, trs, out_tr.at[c]).wait()

        def both():
            for k in range(2):
                got(out_tr.at[k], "tr", off=k)

        at_home(mine)
        at_away(both)
        for k in range(2, 8):
            got(out_tr.at[k], "tr", off=k)

    barrier = pltpu.get_barrier_semaphore()
    peers = [dev(x, yp, z, c), dev(x, ym, z, c)]
    peers += [dev(x, y, z_, c_) for z_ in (zp, zm) for c_ in (0, 1)]
    for x_ in (x, xp, xm, xq):
        for z_ in (z, zq):
            for c_ in (c, 1 - c):
                if not (x_ is x and z_ is z and c_ is c):
                    peers.append(dev(x_, y, z_, c_))
    for peer in peers:
        pl.semaphore_signal(barrier, inc=1, device_id=peer, device_id_type=MESH)

    at_home(lambda: [local(20 + i, panel.at[cols(i)], bs[i].at[r]).start() for i in range(nk)] and None)
    at_home(lambda: local(0, sigma, own_piece).start())

    def structure_out():
        rows = lax.broadcasted_iota(jnp.int32, st_v.shape, 0)
        cols = lax.broadcasted_iota(jnp.int32, st_v.shape, 1)
        v = jnp.zeros(st_v.shape, jnp.int32)
        for i in range(ns):
            for t in range(4):
                v = jnp.where((rows == i) & (cols == t), struct[i, t], v)
        st_v[...] = v

    at_home(structure_out)
    pl.semaphore_wait(barrier, len(peers))

    az_send()
    at_away(az_own_away)
    at_home(lambda: go("home", lambda: remote(st_v, st_v, ("st",), ("st",), sib)))
    last = [i for i in range(nk) if chunks[i][0] == ns - 1]
    early = [i for i in range(nk) if i not in last]
    first = [i for i in early if chunks[i][0] == 0]
    middle = [i for i in early if i not in first]

    def own_from_home(i):
        local(20 + i, panel.at[cols(i)], bs[i].at[r]).wait()
        x_own("home", i)

    def home_start():
        for i in early:
            own_from_home(i)
        local(0, sigma, own_piece).wait()
        got(sig.at[4 * y + 2 * zl + 1 - c], "az_own")
        ay_send("home", 0)
        local(1, dq, dqv).start()
        local(2, dqd, dqd_v).start()
        go("home", lambda: remote(dqd, dqd_v, ("dqd",), ("dqd",), sib))

    at_home(home_start)
    local(4, dinv, dinv_v).start()
    local(5, dqd, own_v).start()
    az_near()

    def home_1():
        ay_send("home", 1)
        for i in first:
            x_forward("home", i)

    def own_from_away(i):
        sw_got(PANEL, i)
        x_own("away", i)

    def away_1():
        ay_send("away", 0)
        az_far()
        for i in range(nk):
            sw_send(PANEL, i)
        ay_send("away", 1)
        for i in range(ns):
            sw_send(DQ, i)
        for i in first:
            own_from_away(i)

    at_home(home_1)
    at_away(away_1)
    ay_forward(0)

    def home_2():
        for i in middle:
            x_forward("home", i)
        for i in last:
            own_from_home(i)
        for i in first:
            x_far("home", i)

    def away_2():
        for i in middle:
            own_from_away(i)
        for i in first:
            x_forward("away", i)

    at_home(home_2)
    at_away(away_2)
    ay_forward(1)

    def home_3():
        for i in middle:
            x_far("home", i)
        local(1, dq, dqv).wait()
        local(2, dqd, dqd_v).wait()
        for i in last:
            x_forward("home", i)
        for i in last:
            x_far("home", i)

    def away_3():
        for i in last:
            own_from_away(i)
        for i in middle:
            x_forward("away", i)
        got(dqd_v, "dqd")
        got(st_v, "st")
        for i in first:
            x_far("away", i)
        sw_got(DQ, 0)

    at_home(home_3)
    at_away(away_3)
    own_trace()
    cp = local(3, st_v, st_s)
    cp.start()
    cp.wait()
    trs[...] = jnp.zeros_like(trs)
    ay_done()
    ahead = list(last)
    for i in first:
        x_sib(i)
        compute(i)
        if ahead:
            at_away(lambda: x_forward("away", ahead[0]))
            ahead.pop(0)
    for i in ahead:
        at_away(lambda i=i: x_forward("away", i))
    for i in first:
        rs_a(i)

    def away_4():
        for i in middle:
            x_far("away", i)
        for i in range(1, ns - 1):
            sw_got(DQ, i)

    at_away(away_4)
    for i in middle:
        x_sib(i)
        compute(i)
    for i in first:
        rs_b(i)

    def away_5():
        sw_got(DQ, ns - 1)
        x_far("away", last[0])

    at_away(away_5)
    for i in middle:
        rs_a(i)
    for j, i in enumerate(last):
        x_sib(i)
        compute(i)
        if j + 1 < len(last):
            at_away(lambda j=j: x_far("away", last[j + 1]))
    trace_send()
    for i in middle:
        rs_b(i)
    for i in last:
        rs_a(i)
    for i in first:
        rs_c(i)
    for i in last:
        rs_b(i)
    for i in middle:
        rs_c(i)
    for i in last:
        rs_c(i)

    def home_end():
        for i in range(nk):
            s, off, wc = chunks[i]
            local(10 + i, cbuf.at[cols(i)], out_panel.at[cols(i)]).wait()
            part = pl.ds(off, wc)
            local(26 + i, fsrc.at[s, :, part], out_sum.at[s, :, part]).wait()
        for role, make in sent:
            if role == "home":
                make().wait_send()

    def away_end():
        for i in range(nk):
            s, off, wc = chunks[i]
            sw_got(SEL, i)
            got(out_sum.at[s, :, pl.ds(off, wc)], "rs3", i)
        for role, make in sent:
            if role == "away":
                make().wait_send()

    for role, make in sent:
        if role == "all":
            make().wait_send()
    at_home(home_end)
    at_away(away_end)
    trace_got()


def write_kernel(ns, p_in, sum_in, tr_in, dinv, p_out, diag_out, tr_out, pv, sv, tv, dv, ov, sem):
    row = lax.axis_index("row")
    share = sv.shape[1]
    mine = pl.ds(pl.multiple_of(row * share, share), share)

    def copy(i, src, dst):
        return pltpu.make_async_copy(src, dst, sem.at[i])

    rest = [(ns, sum_in, sv), (ns + 1, dinv.at[:, mine], dv), (ns + 2, tr_in, tv)]
    for i, src, dst in rest:
        copy(i, src, dst).start()
    for i in range(ns):
        copy(i, p_in.at[i], pv.at[i]).start()
    for i, src, dst in rest[:2]:
        copy(i, src, dst).wait()
    ov[...] = dv[...].astype(jnp.float32) + sv[...]
    copy(ns + 3, ov, diag_out).start()
    for i in range(ns):
        copy(i, p_in.at[i], pv.at[i]).wait()
        copy(ns + 4 + i, pv.at[i], p_out.at[i]).start()
    i, src, dst = rest[2]
    copy(i, src, dst).wait()
    total = tv[0]
    for k in range(1, 9):
        total += tv[k]
    for i in range(ns):
        tr_out[i] = jnp.sum(total[i : i + 1, :1])
    for i in range(ns):
        copy(ns + 4 + i, pv.at[i], p_out.at[i]).wait()
    copy(ns + 3, ov, diag_out).wait()


def local(sigma_anc, panel, structure, d_inv, dq_panel, dq_diag):
    ns, w = panel.shape[0], panel.shape[2]
    share = w // 8
    chunks = chunks_of(ns, w)
    slots = all_slots(ns, len(chunks))[2]
    bf, f32 = jnp.bfloat16, jnp.float32
    hbm = pl.BlockSpec(memory_space=pl.ANY)
    smem = pl.BlockSpec(memory_space=pltpu.SMEM)
    found, sums, tr = pl.pallas_call(
        functools.partial(kernel, chunks),
        out_shape=(
            jax.ShapeDtypeStruct((ns, w, w), bf),
            jax.ShapeDtypeStruct((ns, share, w), f32),
            jax.ShapeDtypeStruct((9, 8, 128), f32),
        ),
        in_specs=[smem] + [hbm] * 5,
        out_specs=(hbm, hbm, hbm),
        scratch_shapes=[
            pltpu.VMEM((16, w, w // 2), bf),
            *[pltpu.VMEM((8, w, wc), bf) for _, _, wc in chunks],
            pltpu.VMEM((w, w), f32),
            pltpu.VMEM((ns, w, w), bf),
            pltpu.VMEM((ns, w, w), bf),
            pltpu.VMEM((ns, 2, 4, share, w), f32),
            pltpu.VMEM((ns, 4, share, w), f32),
            pltpu.VMEM((ns, 4, share, w), f32),
            pltpu.VMEM((ns, 2, share // 2, w), f32),
            pltpu.VMEM((ns, 2, share, w), f32),
            pltpu.VMEM((ns, share, w), f32),
            pltpu.VMEM((ns, w, w), bf),
            pltpu.VMEM((ns, w, w), bf),
            pltpu.VMEM((ns, w, w), bf),
            pltpu.VMEM((8, 128), f32),
            pltpu.VMEM((8, 128), f32),
            pltpu.VMEM((8, 128), jnp.int32),
            pltpu.SMEM((8, 128), jnp.int32),
            pltpu.SemaphoreType.DMA((slots,)),
            pltpu.SemaphoreType.DMA((slots,)),
            pltpu.SemaphoreType.DMA((32,)),
        ],
        compiler_params=pltpu.CompilerParams(
            collective_id=0, has_side_effects=True, vmem_limit_bytes=60 * 1024 * 1024
        ),
        name="selected_inverse",
    )(structure, sigma_anc, panel, dq_panel, dq_diag, d_inv)
    return pl.pallas_call(
        functools.partial(write_kernel, ns),
        out_shape=(
            jax.ShapeDtypeStruct((ns, w, w), bf),
            jax.ShapeDtypeStruct((ns, share, w), f32),
            jax.ShapeDtypeStruct((ns,), f32),
        ),
        in_specs=[hbm] * 4,
        out_specs=(hbm, hbm, smem),
        scratch_shapes=[
            pltpu.VMEM((ns, w, w), bf),
            pltpu.VMEM((ns, share, w), f32),
            pltpu.VMEM((9, 8, 128), f32),
            pltpu.VMEM((ns, share, w), bf),
            pltpu.VMEM((ns, share, w), f32),
            pltpu.SemaphoreType.DMA((2 * ns + 4,)),
        ],
        compiler_params=pltpu.CompilerParams(vmem_limit_bytes=60 * 1024 * 1024),
        name="write_results",
    )(found, sums, tr, d_inv)


def solution(mesh):
    return jax.shard_map(
        local,
        mesh=mesh,
        in_specs=(
            P("row", "col"),
            P("col", "row", None),
            P("col", None),
            P("col", None, None),
            P("col", "row", None),
            P("col", None, None),
        ),
        out_specs=(P("col", "row", None), P("col", "row", None), P("col")),
        check_vma=False,
    )
```

```python
import functools

import jax
import jax.numpy as jnp
from jax import lax
from jax.experimental import pallas as pl
from jax.experimental.pallas import tpu as pltpu
from jax.sharding import PartitionSpec as P

MESH = pl.DeviceIdType.MESH
PANEL, DQ, SEL = 0, 1, 2
SPLIT = (2, 1, 2)


def chunks_of(ns, w):
    out = []
    for i in range(ns):
        n = SPLIT[i % len(SPLIT)]
        out += [(i, j * (w // n), w // n) for j in range(n)]
    return out


class Slots:
    def __init__(self):
        self.at = {}

    def __call__(self, *name, span=1):
        if name not in self.at:
            self.at[name] = sum(self.size.values()) if hasattr(self, "size") else 0
            self.size = getattr(self, "size", {})
            self.size[name] = span
        return self.at[name]


def all_slots(ns, nk):
    send, recv = Slots(), Slots()
    for name in ("pieces", "piece", "panel", "dq", "selected", "sums", "tiles", "tile", "small", "st", "dqd", "dinv"):
        send(name)
    for i in range(nk):
        send("x", i)
        send("rs", i)
    for name in ("st", "dqd", "dinv", "az_own", "az_nb", "az_far", "ayf", "selected", "sums", "tiles", "trz"):
        recv(name)
    for d in range(2):
        for j in range(2):
            recv("ay", d, j)
        for i in range(nk):
            recv("xo", d, i)
    for i in range(nk):
        for name in ("xf", "xs", "rs1", "rsa", "rsb", "panel"):
            recv(name, i)
    for i in range(ns):
        recv("dq", i)
    return send, recv, sum(send.size.values()), sum(recv.size.values())


def kernel(
    chunks, struct, sigma, panel, dq, dqd, dinv,
    out_panel, out_sum, out_tr,
    sig, *rest,
):
    nk = len(chunks)
    ns = chunks[-1][0] + 1
    bs = rest[:nk]
    (dqv, cbuf, ip, rk, sx, ra, rr, fsrc, dqd_v, dinv_v, dinv_r, own_v, td, trs, tra, tsum, st_v, st_s, st_in,
     send_sem, recv_sem, loc_sem) = rest[nk + 1 :]
    prod = rest[nk]
    w = dqv.shape[1]
    hw = w // 2
    share = w // 8
    send_at, recv_at = all_slots(ns, nk)[:2]

    row, col = lax.axis_index("row"), lax.axis_index("col")
    x, zh = row // 2, row % 2
    y, zl, c = col // 4, (col // 2) % 2, col % 2
    z = zh * 2 + zl
    home = c == zh
    hb = 1 - (c + zh) % 2
    r = 2 * x + c
    xp, xm, xq = (x + 1) % 4, (x + 3) % 4, (x + 2) % 4
    yp, ym, yq = (y + 1) % 4, (y + 3) % 4, (y + 2) % 4
    zp, zm, zq = (z + 1) % 4, (z + 3) % 4, (z + 2) % 4

    def dev(x_, y_, z_, c_):
        return (x_ * 2 + z_ // 2, (y_ * 2 + z_ % 2) * 2 + c_)

    sib = dev(x, y, z, 1 - c)
    partner = dev(x, y, zq, 1 - c)


    def go(src, dst, sname, rname, to):
        pltpu.make_async_remote_copy(
            src_ref=src,
            dst_ref=dst,
            send_sem=send_sem.at[send_at(*sname)],
            recv_sem=recv_sem.at[recv_at(*rname)],
            device_id=to,
            device_id_type=MESH,
        ).start()

    def got(dst, *name):
        pltpu.make_async_copy(dst, dst, recv_sem.at[recv_at(*name)]).wait()

    def gone(src, *name):
        pltpu.make_async_copy(src, src, send_sem.at[send_at(*name)]).wait()

    def local(i, src, dst):
        return pltpu.make_async_copy(src, dst, loc_sem.at[i])

    def at_home(f):
        pl.when(home)(f)

    def at_away(f):
        pl.when(jnp.logical_not(home))(f)

    own_piece = sig.at[4 * y + 2 * zl + c]

    def az_send():
        for z_, name in ((zp, "az_nb"), (zm, "az_nb"), (zq, "az_far")):
            go(sigma, own_piece, ("pieces",), (name,), dev(x, y, z_, zh))

    def az_own_away():
        go(sigma, own_piece, ("piece",), ("az_own",), sib)

    def az_near():
        got(sig.at[pl.ds(4 * y + 2 * (1 - zl), 2)], "az_nb")

    def az_far():
        got(sig.at[pl.ds(4 * y + 2 * zl, 2)], "az_far")

    pair_zl = ((zl * hb + (1 - zl) * (1 - hb)), ((1 - zl) * hb + zl * (1 - hb)))

    def pair(y_, j):
        return sig.at[pl.ds(4 * y_ + 2 * pair_zl[j], 2)]

    def ay_send(j):
        go(pair(y, j), pair(y, j), ("pieces",), ("ay", 0, j), dev(x, yp, z, c))
        go(pair(y, j), pair(y, j), ("pieces",), ("ay", 1, j), dev(x, ym, z, c))

    def ay_forward(j):
        got(pair(ym, j), "ay", 0, j)
        p0 = sig.at[4 * ym + 2 * pair_zl[j]]
        go(p0, p0, ("pieces",), ("ayf",), dev(x, yp, z, c))
        got(pair(yp, j), "ay", 1, j)
        p1 = sig.at[4 * yp + 2 * pair_zl[j] + 1]
        go(p1, p1, ("pieces",), ("ayf",), dev(x, ym, z, c))

    def ay_done():
        got(sig.at[pl.ds(4 * yq, 4)], "ayf")

    def blk(i, x_, c_=None):
        return bs[i].at[2 * x_ + (c if c_ is None else c_)]

    def half(i, x_, d):
        return bs[i].at[2 * x_ + c, pl.ds(d * hw, hw)]

    def to_sib(i, x_):
        go(blk(i, x_), blk(i, x_), ("x", i), ("xs", i), sib)

    def x_own(i):
        go(blk(i, x), blk(i, x), ("x", i), ("xo", 0, i), dev(xp, y, z, c))
        go(blk(i, x), blk(i, x), ("x", i), ("xo", 1, i), dev(xm, y, z, c))
        to_sib(i, x)

    def x_forward(i):
        got(blk(i, xm), "xo", 0, i)
        go(half(i, xm, 0), half(i, xm, 0), ("x", i), ("xf", i), dev(xp, y, z, c))
        got(blk(i, xp), "xo", 1, i)
        go(half(i, xp, 1), half(i, xp, 1), ("x", i), ("xf", i), dev(xm, y, z, c))
        to_sib(i, xm)
        to_sib(i, xp)

    def x_far(i):
        got(blk(i, xq), "xf", i)
        to_sib(i, xq)

    def x_sib(i):
        got(bs[i].at[pl.ds(0, 4)], "xs", i)

    def cols(i):
        return chunks[i][0], slice(None), pl.ds(chunks[i][1], chunks[i][2])

    def sw_dst(kind, i, r_):
        if kind == PANEL:
            return bs[i].at[r_]
        return dqv.at[i] if kind == DQ else out_panel.at[cols(i)]

    def sw_send(kind, i):
        src = panel.at[cols(i)] if kind == PANEL else dq.at[i] if kind == DQ else cbuf.at[cols(i)]
        name = ("panel", "dq", "selected")[kind]
        go(src, sw_dst(kind, i, 2 * x + 1 - c), (name,), (name,) if kind == SEL else (name, i), partner)

    def sw_got(kind, i):
        got(sw_dst(kind, i, r), ("panel", "dq")[kind], i)

    def compute(i):
        b = bs[i]
        s, off, wc = chunks[i]
        lanes = slice(off, off + wc)

        def step(t, carry):
            k = st_s[s, t]
            v = jnp.dot(sig[2 * k], b[k, :hw], preferred_element_type=jnp.float32)
            v += jnp.dot(sig[2 * k + 1], b[k, hw:], preferred_element_type=jnp.float32)
            prod[:, :wc] += v
            return carry

        prod[:, :wc] = jnp.zeros((w, wc), jnp.float32)
        lax.fori_loop(0, 4, step, 0)
        here = jnp.float32(0)
        for t in range(4):
            here += jnp.where(st_s[s, t] == r, jnp.float32(1), jnp.float32(0))
        kept = prod[:, :wc] * here
        hi = kept.astype(jnp.bfloat16)
        cbuf[s, :, lanes] = -hi

        def selected_home():
            local(10 + i, cbuf.at[cols(i)], out_panel.at[cols(i)]).start()

        at_home(selected_home)
        at_away(lambda: sw_send(SEL, i))
        lo = (kept - hi.astype(jnp.float32)).astype(jnp.bfloat16)
        trace = -2.0 * jnp.sum(kept * dqv[s, :, lanes].astype(jnp.float32), axis=0, keepdims=True)
        for i2, (s2, off2, wc2) in enumerate(chunks):
            if s2 != s:
                continue
            own = bs[i2][r]
            inner = lax.dot_general(own, hi, (((0,), (0,)), ((), ())), preferred_element_type=jnp.float32)
            inner += lax.dot_general(own, lo, (((0,), (0,)), ((), ())), preferred_element_type=jnp.float32)
            for a in range(wc2 // share):
                a2 = off2 // share + a
                ip[s, 4 * (a2 % 2) + a2 // 2, :, lanes] = inner[a * share : (a + 1) * share]
            weight = dqd_v[s, off2 : off2 + wc2, lanes].astype(jnp.float32)
            trace += jnp.sum(inner * weight, axis=0, keepdims=True)
        part = pl.ds(off, wc)
        go(ip.at[s, pl.ds(4 * (1 - c), 4), :, part], rk.at[s, :, :, part], ("rs", i), ("rs1", i), sib)
        trs[s : s + 1, :] += jnp.broadcast_to(jnp.sum(trace, axis=1, keepdims=True), (1, 128))

    hs = share // 2
    near = (xp, xm)

    def rs_a(i):
        s, off, wc = chunks[i]
        lanes, part = slice(off, off + wc), pl.ds(off, wc)
        got(rk.at[s, :, :, part], "rs1", i)
        sx[s, :, :, lanes] = ip[s, pl.ds(4 * c, 4), :, lanes] + rk[s, :, :, lanes]
        for d in range(2):
            go(sx.at[s, xq, pl.ds(d * hs, hs), part], ra.at[s, d, :, part], ("rs", i), ("rsa", i),
               dev(near[d], y, z, c))

    def rs_b(i):
        s, off, wc = chunks[i]
        lanes, part = slice(off, off + wc), pl.ds(off, wc)
        got(ra.at[s, :, :, part], "rsa", i)
        for d in range(2):
            sx[s, near[d], d * hs : (d + 1) * hs, lanes] += ra[s, d, :, lanes]
            go(sx.at[s, near[d], :, part], rr.at[s, d, :, part], ("rs", i), ("rsb", i), dev(near[d], y, z, c))

    def rs_c(i):
        s, off, wc = chunks[i]
        lanes, part = slice(off, off + wc), pl.ds(off, wc)
        got(rr.at[s, :, :, part], "rsb", i)
        total = sx[s, x, :, lanes] + rr[s, 0, :, lanes] + rr[s, 1, :, lanes]
        fsrc[s, :, lanes] = dinv_r[s, :, lanes].astype(jnp.float32) + total

        at_home(lambda: local(26 + i, fsrc.at[s, :, part], out_sum.at[s, :, part]).start())
        at_away(lambda: go(fsrc.at[s, :, part], out_sum.at[s, :, part], ("sums",), ("sums",), partner))

    def own_trace():
        local(4, dinv, dinv_v).wait()
        local(5, dqd, own_v).wait()
        td[...] = jnp.zeros_like(td)
        for i in range(ns):
            v = jnp.sum(dinv_v[i].astype(jnp.float32) * own_v[i].astype(jnp.float32), axis=0, keepdims=True)
            td[i : i + 1, :] = jnp.broadcast_to(jnp.sum(v, axis=1, keepdims=True), (1, 128))
        local(6, td, out_tr.at[1]).start()

    def trace_send():
        def tile(dx, name):
            go(trs, tra.at[2 * dx + c], (name,), ("tiles",), dev((x + dx) % 4, y, z, zh))

        at_away(lambda: tile(0, "tile"))
        at_home(keep_tile)
        for dx in range(1, 4):
            tile(dx, "tiles")

    def keep_tile():
        tsum[...] = trs[...]

    def trace_sum():
        got(tra.at[pl.ds(0, 7)], "tiles")
        total = tsum[...]
        for k in range(2, 8):
            total += tra[k]
        tsum[...] = total + tra[1 - c]
        local(8, tsum, out_tr.at[0]).start()
        go(tsum, out_tr.at[0], ("small",), ("trz",), dev(x, y, zq, c))

    def trace_got():
        local(6, td, out_tr.at[1]).wait()
        at_home(lambda: local(8, tsum, out_tr.at[0]).wait())
        at_away(lambda: got(out_tr.at[0], "trz"))

    barrier = pltpu.get_barrier_semaphore()
    peers = [dev(x, yp, z, c), dev(x, ym, z, c), sib]
    for c_ in (0, 1):
        peers += [dev(x_, y, z, c_) for x_ in (xp, xm, xq)]
        peers += [dev(x, y, z_, c_) for z_ in (zp, zm, zq)]
    for peer in peers:
        pl.semaphore_signal(barrier, inc=1, device_id=peer, device_id_type=MESH)

    at_home(lambda: [local(20 + i, panel.at[cols(i)], bs[i].at[r]).start() for i in range(nk)] and None)
    at_home(lambda: local(0, sigma, own_piece).start())
    at_home(lambda: local(7, struct, st_in).start())

    def structure_out():
        rows = lax.broadcasted_iota(jnp.int32, st_v.shape, 0)
        lanes = lax.broadcasted_iota(jnp.int32, st_v.shape, 1)
        local(7, struct, st_in).wait()
        v = jnp.zeros(st_v.shape, jnp.int32)
        for i in range(ns):
            for t in range(4):
                v = jnp.where((rows == i) & (lanes == t), st_in[i, t], v)
        st_v[...] = v

    at_home(structure_out)
    pl.semaphore_wait(barrier, len(peers))

    az_send()
    at_away(az_own_away)
    at_home(lambda: go(st_v, st_v, ("st",), ("st",), sib))
    last = [i for i in range(nk) if chunks[i][0] == ns - 1]
    early = [i for i in range(nk) if i not in last]
    first = [i for i in early if chunks[i][0] == 0]
    middle = [i for i in early if i not in first]

    def own_from_home(i):
        local(20 + i, panel.at[cols(i)], bs[i].at[r]).wait()
        x_own(i)

    def d_rows(r_):
        return dinv.at[:, pl.ds(pl.multiple_of(r_ * share, share), share)]

    def home_start():
        for i in early:
            own_from_home(i)
        local(0, sigma, own_piece).wait()
        got(own_piece, "az_own")
        ay_send(0)
        local(1, dq, dqv).start()
        local(2, dqd, dqd_v).start()
        go(dqd, dqd_v, ("dqd",), ("dqd",), sib)
        local(9, d_rows(r), dinv_r).start()
        go(d_rows(2 * x + 1 - c), dinv_r, ("dinv",), ("dinv",), sib)

    at_home(home_start)
    local(4, dinv, dinv_v).start()
    local(5, dqd, own_v).start()
    az_near()

    def home_1():
        ay_send(1)
        for i in first:
            x_forward(i)

    def own_from_away(i):
        sw_got(PANEL, i)
        x_own(i)

    def away_1():
        ay_send(0)
        az_far()
        for i in range(nk):
            sw_send(PANEL, i)
        ay_send(1)
        for i in range(ns):
            sw_send(DQ, i)
        for i in first:
            own_from_away(i)

    at_home(home_1)
    at_away(away_1)
    ay_forward(0)

    def home_2():
        for i in middle:
            x_forward(i)
        for i in last:
            own_from_home(i)
        for i in first:
            x_far(i)

    def away_2():
        for i in middle:
            own_from_away(i)
        for i in first:
            x_forward(i)

    at_home(home_2)
    at_away(away_2)
    ay_forward(1)

    def home_3():
        for i in middle:
            x_far(i)
        local(1, dq, dqv).wait()
        local(2, dqd, dqd_v).wait()
        local(9, d_rows(r), dinv_r).wait()
        for i in last:
            x_forward(i)
        for i in last:
            x_far(i)

    def away_3():
        for i in last:
            own_from_away(i)
        for i in middle:
            x_forward(i)
        got(dqd_v, "dqd")
        got(dinv_r, "dinv")
        got(st_v, "st")
        for i in first:
            x_far(i)
        sw_got(DQ, 0)

    at_home(home_3)
    at_away(away_3)
    own_trace()
    cp = local(3, st_v, st_s)
    cp.start()
    cp.wait()
    trs[...] = jnp.zeros_like(trs)
    ay_done()
    ahead = list(last)
    for i in first:
        x_sib(i)
        compute(i)
        if ahead:
            at_away(lambda: x_forward(ahead[0]))
            ahead.pop(0)
    for i in ahead:
        at_away(lambda i=i: x_forward(i))
    for i in first:
        rs_a(i)

    def away_4():
        for i in middle:
            x_far(i)
        for i in range(1, ns - 1):
            sw_got(DQ, i)

    at_away(away_4)
    for i in middle:
        x_sib(i)
        compute(i)
    for i in first:
        rs_b(i)

    def home_5():
        for i in middle:
            rs_a(i)

    def away_5():
        sw_got(DQ, ns - 1)
        x_far(last[0])

    at_home(home_5)
    at_away(away_5)
    x_sib(last[0])
    compute(last[0])

    def away_6():
        for i in last[1:]:
            x_far(i)
        for i in middle:
            rs_a(i)

    at_away(away_6)
    for i in last[1:]:
        x_sib(i)
        compute(i)
    trace_send()

    for i in middle:
        rs_b(i)
    for i in first:
        rs_c(i)
    for i in last:
        rs_a(i)
    rs_b(last[0])
    for i in last[1:]:
        rs_b(i)
    for i in middle:
        rs_c(i)
    at_home(trace_sum)
    for i in last:
        rs_c(i)

    def home_end():
        for i in range(nk):
            s, off, wc = chunks[i]
            local(10 + i, cbuf.at[cols(i)], out_panel.at[cols(i)]).wait()
            part = pl.ds(off, wc)
            local(26 + i, fsrc.at[s, :, part], out_sum.at[s, :, part]).wait()
        gone(st_v, "st")
        gone(dqd, "dqd")
        gone(dinv_r, "dinv")
        gone(tsum, "small")

    def away_end():
        gone(own_piece, "piece")
        gone(panel, "panel")
        gone(dq, "dq")
        gone(cbuf, "selected")
        gone(fsrc, "sums")
        gone(trs, "tile")
        got(out_panel, "selected")
        got(out_sum, "sums")

    gone(sig.at[pl.ds(0, 15)], "pieces")
    for i in range(nk):
        s, off, wc = chunks[i]
        gone(bs[i].at[pl.ds(0, 7)], "x", i)
        gone(ip.at[s, pl.ds(0, 7), :, pl.ds(off, wc)], "rs", i)
    gone(tra.at[pl.ds(0, 3)], "tiles")
    at_home(home_end)
    at_away(away_end)
    trace_got()


def write_kernel(p_in, diag_in, tr_in, p_out, diag_out, tr_out, tv, sem):
    ns = p_in.shape[0]
    copies = [
        pltpu.make_async_copy(src, dst, sem.at[i])
        for i, (src, dst) in enumerate(((tr_in, tv), (p_in, p_out), (diag_in, diag_out)))
    ]
    for copy in copies:
        copy.start()
    copies[0].wait()
    total = tv[0] + tv[1]
    for i in range(ns):
        tr_out[i] = jnp.sum(total[i : i + 1, :1])
    copies[1].wait()
    copies[2].wait()


def local(sigma_anc, panel, structure, d_inv, dq_panel, dq_diag):
    ns, w = panel.shape[0], panel.shape[2]
    share = w // 8
    chunks = chunks_of(ns, w)
    n_send, n_recv = all_slots(ns, len(chunks))[2:]
    bf, f32 = jnp.bfloat16, jnp.float32
    anywhere = pl.BlockSpec(memory_space=pl.ANY)
    hbm = pl.BlockSpec(memory_space=pltpu.HBM)
    smem = pl.BlockSpec(memory_space=pltpu.SMEM)
    found, sums, tr = pl.pallas_call(
        functools.partial(kernel, chunks),
        out_shape=(
            jax.ShapeDtypeStruct((ns, w, w), bf),
            jax.ShapeDtypeStruct((ns, share, w), f32),
            jax.ShapeDtypeStruct((2, 8, 128), f32),
        ),
        in_specs=[hbm] * 6,
        out_specs=(anywhere, anywhere, anywhere),
        scratch_shapes=[
            pltpu.VMEM((16, w, w // 2), bf),
            *[pltpu.VMEM((8, w, wc), bf) for _, _, wc in chunks],
            pltpu.VMEM((w, w), f32),
            pltpu.VMEM((ns, w, w), bf),
            pltpu.VMEM((ns, w, w), bf),
            pltpu.VMEM((ns, 8, share, w), f32),
            pltpu.VMEM((ns, 4, share, w), f32),
            pltpu.VMEM((ns, 4, share, w), f32),
            pltpu.VMEM((ns, 2, share // 2, w), f32),
            pltpu.VMEM((ns, 2, share, w), f32),
            pltpu.VMEM((ns, share, w), f32),
            pltpu.VMEM((ns, w, w), bf),
            pltpu.VMEM((ns, w, w), bf),
            pltpu.VMEM((ns, share, w), bf),
            pltpu.VMEM((ns, w, w), bf),
            pltpu.VMEM((8, 128), f32),
            pltpu.VMEM((8, 128), f32),
            pltpu.VMEM((8, 8, 128), f32),
            pltpu.VMEM((8, 128), f32),
            pltpu.VMEM((8, 128), jnp.int32),
            pltpu.SMEM((8, 128), jnp.int32),
            pltpu.SMEM(structure.shape, jnp.int32),
            pltpu.SemaphoreType.DMA((n_send,)),
            pltpu.SemaphoreType.DMA((n_recv,)),
            pltpu.SemaphoreType.DMA((32,)),
        ],
        compiler_params=pltpu.CompilerParams(
            collective_id=0, has_side_effects=True, vmem_limit_bytes=44 * 1024 * 1024
        ),
        name="selected_inverse",
    )(*(pltpu.with_memory_space_constraint(v, pltpu.HBM) for v in (structure, sigma_anc, panel, dq_panel, dq_diag, d_inv)))
    return pl.pallas_call(
        write_kernel,
        out_shape=(
            jax.ShapeDtypeStruct((ns, w, w), bf),
            jax.ShapeDtypeStruct((ns, share, w), f32),
            jax.ShapeDtypeStruct((ns,), f32),
        ),
        in_specs=[anywhere] * 3,
        out_specs=(hbm, hbm, smem),
        scratch_shapes=[
            pltpu.VMEM((2, 8, 128), f32),
            pltpu.SemaphoreType.DMA((3,)),
        ],
        compiler_params=pltpu.CompilerParams(vmem_limit_bytes=4 * 1024 * 1024),
        name="write_results",
    )(found, sums, tr)


def solution(mesh):
    return jax.shard_map(
        local,
        mesh=mesh,
        in_specs=(
            P("row", "col"),
            P("col", "row", None),
            P("col", None),
            P("col", None, None),
            P("col", "row", None),
            P("col", None, None),
        ),
        out_specs=(P("col", "row", None), P("col", "row", None), P("col")),
        check_vma=False,
    )
```

```python
import functools

import jax
import jax.numpy as jnp
from jax import lax
from jax.experimental import pallas as pl
from jax.experimental.pallas import tpu as pltpu
from jax.sharding import PartitionSpec as P

MESH = pl.DeviceIdType.MESH
PANEL, DQ, SEL = 0, 1, 2
SPLIT = (2, 2, 2)


def chunks_of(ns, w):
    out = []
    for i in range(ns):
        n = SPLIT[i % len(SPLIT)]
        out += [(i, j * (w // n), w // n) for j in range(n)]
    return out


class Slots:
    def __init__(self):
        self.at = {}

    def __call__(self, *name, span=1):
        if name not in self.at:
            self.at[name] = sum(self.size.values()) if hasattr(self, "size") else 0
            self.size = getattr(self, "size", {})
            self.size[name] = span
        return self.at[name]


def all_slots(ns, nk):
    send, recv = Slots(), Slots()
    for name in ("pieces", "piece", "panel", "dq", "selected", "sums", "tiles", "tile", "small", "st", "dqd", "dinv"):
        send(name)
    for i in range(nk):
        send("x", i)
        send("rs", i)
    for name in ("st", "dqd", "dinv", "az_own", "az_nb", "az_far", "ayf", "selected", "sums", "tiles", "trz"):
        recv(name)
    for d in range(2):
        for j in range(2):
            recv("ay", d, j)
        for i in range(nk):
            recv("xo", d, i)
    for i in range(nk):
        for name in ("xf", "xs", "rs1", "rsa", "rsb", "panel"):
            recv(name, i)
    for i in range(ns):
        recv("dq", i)
    return send, recv, sum(send.size.values()), sum(recv.size.values())


def kernel(
    chunks, struct, sigma, panel, dq, dqd, dinv,
    out_panel, out_sum, out_tr,
    sig, *rest,
):
    nk = len(chunks)
    ns = chunks[-1][0] + 1
    bs = rest[:nk]
    (dqv, cbuf, own_t, ip, rk, sx, ra, rr, fsrc, dqd_v, dinv_v, dinv_r, own_v, td, trs, tra, tsum, st_v, st_s, st_in,
     send_sem, recv_sem, loc_sem) = rest[nk + 1 :]
    prod = rest[nk]
    w = dqv.shape[1]
    hw = w // 2
    share = w // 8
    send_at, recv_at = all_slots(ns, nk)[:2]

    row, col = lax.axis_index("row"), lax.axis_index("col")
    x, zh = row // 2, row % 2
    y, zl, c = col // 4, (col // 2) % 2, col % 2
    z = zh * 2 + zl
    home = c == zh
    hb = 1 - (c + zh) % 2
    r = 2 * x + c
    xp, xm, xq = (x + 1) % 4, (x + 3) % 4, (x + 2) % 4
    yp, ym, yq = (y + 1) % 4, (y + 3) % 4, (y + 2) % 4
    zp, zm, zq = (z + 1) % 4, (z + 3) % 4, (z + 2) % 4

    def dev(x_, y_, z_, c_):
        return (x_ * 2 + z_ // 2, (y_ * 2 + z_ % 2) * 2 + c_)

    sib = dev(x, y, z, 1 - c)
    partner = dev(x, y, zq, 1 - c)


    def go(src, dst, sname, rname, to):
        pltpu.make_async_remote_copy(
            src_ref=src,
            dst_ref=dst,
            send_sem=send_sem.at[send_at(*sname)],
            recv_sem=recv_sem.at[recv_at(*rname)],
            device_id=to,
            device_id_type=MESH,
        ).start()

    def got(dst, *name):
        pltpu.make_async_copy(dst, dst, recv_sem.at[recv_at(*name)]).wait()

    def gone(src, *name):
        pltpu.make_async_copy(src, src, send_sem.at[send_at(*name)]).wait()

    def local(i, src, dst):
        return pltpu.make_async_copy(src, dst, loc_sem.at[i])

    def at_home(f):
        pl.when(home)(f)

    def at_away(f):
        pl.when(jnp.logical_not(home))(f)

    own_piece = sig.at[4 * y + 2 * zl + c]

    def az_send():
        for z_, name in ((zp, "az_nb"), (zm, "az_nb"), (zq, "az_far")):
            go(sigma, own_piece, ("pieces",), (name,), dev(x, y, z_, zh))

    def az_own_away():
        go(sigma, own_piece, ("piece",), ("az_own",), sib)

    def az_near():
        got(sig.at[pl.ds(4 * y + 2 * (1 - zl), 2)], "az_nb")

    def az_far():
        got(sig.at[pl.ds(4 * y + 2 * zl, 2)], "az_far")

    pair_zl = ((zl * hb + (1 - zl) * (1 - hb)), ((1 - zl) * hb + zl * (1 - hb)))

    def pair(y_, j):
        return sig.at[pl.ds(4 * y_ + 2 * pair_zl[j], 2)]

    def ay_send(j):
        go(pair(y, j), pair(y, j), ("pieces",), ("ay", 0, j), dev(x, yp, z, c))
        go(pair(y, j), pair(y, j), ("pieces",), ("ay", 1, j), dev(x, ym, z, c))

    def ay_forward(j):
        got(pair(ym, j), "ay", 0, j)
        p0 = sig.at[4 * ym + 2 * pair_zl[j]]
        go(p0, p0, ("pieces",), ("ayf",), dev(x, yp, z, c))
        got(pair(yp, j), "ay", 1, j)
        p1 = sig.at[4 * yp + 2 * pair_zl[j] + 1]
        go(p1, p1, ("pieces",), ("ayf",), dev(x, ym, z, c))

    def ay_done():
        got(sig.at[pl.ds(4 * yq, 4)], "ayf")

    def blk(i, x_, c_=None):
        return bs[i].at[2 * x_ + (c if c_ is None else c_)]

    def half(i, x_, d):
        return bs[i].at[2 * x_ + c, pl.ds(d * hw, hw)]

    def to_sib(i, x_):
        go(blk(i, x_), blk(i, x_), ("x", i), ("xs", i), sib)

    def x_own(i):
        go(blk(i, x), blk(i, x), ("x", i), ("xo", 0, i), dev(xp, y, z, c))
        go(blk(i, x), blk(i, x), ("x", i), ("xo", 1, i), dev(xm, y, z, c))
        to_sib(i, x)

    def x_forward(i):
        got(blk(i, xm), "xo", 0, i)
        go(half(i, xm, 0), half(i, xm, 0), ("x", i), ("xf", i), dev(xp, y, z, c))
        got(blk(i, xp), "xo", 1, i)
        go(half(i, xp, 1), half(i, xp, 1), ("x", i), ("xf", i), dev(xm, y, z, c))
        to_sib(i, xm)
        to_sib(i, xp)

    def x_far(i):
        got(blk(i, xq), "xf", i)
        to_sib(i, xq)

    def x_sib(i):
        got(bs[i].at[pl.ds(0, 4)], "xs", i)

    def cols(i):
        return chunks[i][0], slice(None), pl.ds(chunks[i][1], chunks[i][2])

    def sw_dst(kind, i, r_):
        if kind == PANEL:
            return bs[i].at[r_]
        return dqv.at[i] if kind == DQ else out_panel.at[cols(i)]

    def sw_send(kind, i):
        src = panel.at[cols(i)] if kind == PANEL else dq.at[i] if kind == DQ else cbuf.at[cols(i)]
        name = ("panel", "dq", "selected")[kind]
        go(src, sw_dst(kind, i, 2 * x + 1 - c), (name,), (name,) if kind == SEL else (name, i), partner)

    def sw_got(kind, i):
        got(sw_dst(kind, i, r), ("panel", "dq")[kind], i)

    def turn_own():
        for i, (s, off, wc) in enumerate(chunks):
            own_t[s, off : off + wc, :] = bs[i][r].T

    def compute(i):
        b = bs[i]
        s, off, wc = chunks[i]
        lanes = slice(off, off + wc)

        def step(t, carry):
            k = st_s[s, t]
            v = jnp.dot(sig[2 * k], b[k, :hw], preferred_element_type=jnp.float32)
            v += jnp.dot(sig[2 * k + 1], b[k, hw:], preferred_element_type=jnp.float32)
            prod[:, :wc] += v
            return carry

        prod[:, :wc] = jnp.zeros((w, wc), jnp.float32)
        lax.fori_loop(0, 4, step, 0)
        here = jnp.float32(0)
        for t in range(4):
            here += jnp.where(st_s[s, t] == r, jnp.float32(1), jnp.float32(0))
        kept = prod[:, :wc] * here
        hi = kept.astype(jnp.bfloat16)
        cbuf[s, :, lanes] = -hi

        def selected_home():
            local(10 + i, cbuf.at[cols(i)], out_panel.at[cols(i)]).start()

        at_home(selected_home)
        at_away(lambda: sw_send(SEL, i))
        lo = (kept - hi.astype(jnp.float32)).astype(jnp.bfloat16)
        trace = -2.0 * jnp.sum(kept * dqv[s, :, lanes].astype(jnp.float32), axis=0, keepdims=True)
        inner = jnp.dot(own_t[s], hi, preferred_element_type=jnp.float32)
        inner += jnp.dot(own_t[s], lo, preferred_element_type=jnp.float32)
        for a in range(8):
            ip[s, 4 * (a % 2) + a // 2, :, lanes] = inner[a * share : (a + 1) * share]
        trace += jnp.sum(inner * dqd_v[s, :, lanes].astype(jnp.float32), axis=0, keepdims=True)
        part = pl.ds(off, wc)
        go(ip.at[s, pl.ds(4 * (1 - c), 4), :, part], rk.at[s, :, :, part], ("rs", i), ("rs1", i), sib)
        trs[s : s + 1, :] += jnp.broadcast_to(jnp.sum(trace, axis=1, keepdims=True), (1, 128))

    hs = share // 2
    near = (xp, xm)

    def rs_a(i):
        s, off, wc = chunks[i]
        lanes, part = slice(off, off + wc), pl.ds(off, wc)
        got(rk.at[s, :, :, part], "rs1", i)
        sx[s, :, :, lanes] = ip[s, pl.ds(4 * c, 4), :, lanes] + rk[s, :, :, lanes]
        for d in range(2):
            go(sx.at[s, xq, pl.ds(d * hs, hs), part], ra.at[s, d, :, part], ("rs", i), ("rsa", i),
               dev(near[d], y, z, c))

    def rs_b(i):
        s, off, wc = chunks[i]
        lanes, part = slice(off, off + wc), pl.ds(off, wc)
        got(ra.at[s, :, :, part], "rsa", i)
        for d in range(2):
            sx[s, near[d], d * hs : (d + 1) * hs, lanes] += ra[s, d, :, lanes]
            go(sx.at[s, near[d], :, part], rr.at[s, d, :, part], ("rs", i), ("rsb", i), dev(near[d], y, z, c))

    def rs_c(i):
        s, off, wc = chunks[i]
        lanes, part = slice(off, off + wc), pl.ds(off, wc)
        got(rr.at[s, :, :, part], "rsb", i)
        total = sx[s, x, :, lanes] + rr[s, 0, :, lanes] + rr[s, 1, :, lanes]
        fsrc[s, :, lanes] = dinv_r[s, :, lanes].astype(jnp.float32) + total

        at_home(lambda: local(26 + i, fsrc.at[s, :, part], out_sum.at[s, :, part]).start())
        at_away(lambda: go(fsrc.at[s, :, part], out_sum.at[s, :, part], ("sums",), ("sums",), partner))

    def own_trace():
        local(4, dinv, dinv_v).wait()
        local(5, dqd, own_v).wait()
        td[...] = jnp.zeros_like(td)
        for i in range(ns):
            v = jnp.sum(dinv_v[i].astype(jnp.float32) * own_v[i].astype(jnp.float32), axis=0, keepdims=True)
            td[i : i + 1, :] = jnp.broadcast_to(jnp.sum(v, axis=1, keepdims=True), (1, 128))
        local(6, td, out_tr.at[1]).start()

    def trace_send():
        def tile(dx, name):
            go(trs, tra.at[2 * dx + c], (name,), ("tiles",), dev((x + dx) % 4, y, z, zh))

        at_away(lambda: tile(0, "tile"))
        at_home(keep_tile)
        for dx in range(1, 4):
            tile(dx, "tiles")

    def keep_tile():
        tsum[...] = trs[...]

    def trace_sum():
        got(tra.at[pl.ds(0, 7)], "tiles")
        total = tsum[...]
        for k in range(2, 8):
            total += tra[k]
        tsum[...] = total + tra[1 - c]
        local(8, tsum, out_tr.at[0]).start()
        go(tsum, out_tr.at[0], ("small",), ("trz",), dev(x, y, zq, c))

    def trace_got():
        local(6, td, out_tr.at[1]).wait()
        at_home(lambda: local(8, tsum, out_tr.at[0]).wait())
        at_away(lambda: got(out_tr.at[0], "trz"))

    barrier = pltpu.get_barrier_semaphore()
    peers = [dev(x, yp, z, c), dev(x, ym, z, c), sib]
    for c_ in (0, 1):
        peers += [dev(x_, y, z, c_) for x_ in (xp, xm, xq)]
        peers += [dev(x, y, z_, c_) for z_ in (zp, zm, zq)]
    for peer in peers:
        pl.semaphore_signal(barrier, inc=1, device_id=peer, device_id_type=MESH)

    at_home(lambda: [local(20 + i, panel.at[cols(i)], bs[i].at[r]).start() for i in range(nk)] and None)
    at_home(lambda: local(0, sigma, own_piece).start())
    at_home(lambda: local(7, struct, st_in).start())

    def structure_out():
        rows = lax.broadcasted_iota(jnp.int32, st_v.shape, 0)
        lanes = lax.broadcasted_iota(jnp.int32, st_v.shape, 1)
        local(7, struct, st_in).wait()
        v = jnp.zeros(st_v.shape, jnp.int32)
        for i in range(ns):
            for t in range(4):
                v = jnp.where((rows == i) & (lanes == t), st_in[i, t], v)
        st_v[...] = v

    at_home(structure_out)
    pl.semaphore_wait(barrier, len(peers))

    az_send()
    at_away(az_own_away)
    at_home(lambda: go(st_v, st_v, ("st",), ("st",), sib))
    last = [i for i in range(nk) if chunks[i][0] == ns - 1]
    early = [i for i in range(nk) if i not in last]
    first = [i for i in early if chunks[i][0] == 0]
    middle = [i for i in early if i not in first]

    def own_from_home(i):
        local(20 + i, panel.at[cols(i)], bs[i].at[r]).wait()
        x_own(i)

    def d_rows(r_):
        return dinv.at[:, pl.ds(pl.multiple_of(r_ * share, share), share)]

    def home_start():
        for i in early:
            own_from_home(i)
        local(0, sigma, own_piece).wait()
        got(own_piece, "az_own")
        ay_send(0)
        local(1, dq, dqv).start()
        local(2, dqd, dqd_v).start()
        go(dqd, dqd_v, ("dqd",), ("dqd",), sib)
        local(9, d_rows(r), dinv_r).start()
        go(d_rows(2 * x + 1 - c), dinv_r, ("dinv",), ("dinv",), sib)

    at_home(home_start)
    local(4, dinv, dinv_v).start()
    local(5, dqd, own_v).start()
    az_near()

    def home_1():
        ay_send(1)
        for i in first:
            x_forward(i)

    def own_from_away(i):
        sw_got(PANEL, i)
        x_own(i)

    def away_1():
        ay_send(0)
        az_far()
        for i in range(nk):
            sw_send(PANEL, i)
        ay_send(1)
        for i in range(ns):
            sw_send(DQ, i)
        for i in first:
            own_from_away(i)

    at_home(home_1)
    at_away(away_1)
    ay_forward(0)

    def home_2():
        for i in middle:
            x_forward(i)
        for i in last:
            own_from_home(i)
        for i in first:
            x_far(i)

    def away_2():
        for i in middle:
            own_from_away(i)
        for i in first:
            x_forward(i)

    at_home(home_2)
    at_away(away_2)
    ay_forward(1)

    def home_3():
        for i in middle:
            x_far(i)
        turn_own()
        local(1, dq, dqv).wait()
        local(2, dqd, dqd_v).wait()
        local(9, d_rows(r), dinv_r).wait()
        for i in last:
            x_forward(i)
        for i in last:
            x_far(i)

    def away_3():
        for i in last:
            own_from_away(i)
        turn_own()
        for i in middle:
            x_forward(i)
        got(dqd_v, "dqd")
        got(dinv_r, "dinv")
        got(st_v, "st")
        for i in first:
            x_far(i)
        sw_got(DQ, 0)

    at_home(home_3)
    at_away(away_3)
    own_trace()
    cp = local(3, st_v, st_s)
    cp.start()
    cp.wait()
    trs[...] = jnp.zeros_like(trs)
    ay_done()
    ahead = list(last)
    for i in first:
        x_sib(i)
        compute(i)
        if ahead:
            at_away(lambda: x_forward(ahead[0]))
            ahead.pop(0)
    for i in ahead:
        at_away(lambda i=i: x_forward(i))
    for i in first:
        rs_a(i)

    def away_4():
        for i in range(1, ns - 1):
            sw_got(DQ, i)

    at_away(away_4)
    for i in middle:
        at_away(lambda i=i: x_far(i))
        x_sib(i)
        compute(i)
    for i in first:
        rs_b(i)

    def home_5():
        for i in middle:
            rs_a(i)

    def away_5():
        sw_got(DQ, ns - 1)
        x_far(last[0])

    at_home(home_5)
    at_away(away_5)
    x_sib(last[0])
    compute(last[0])

    def away_6():
        for i in last[1:]:
            x_far(i)
        for i in middle:
            rs_a(i)

    at_away(away_6)
    for i in last[1:]:
        x_sib(i)
        compute(i)
    trace_send()

    for i in last:
        rs_a(i)

    def away_7():
        for i in middle:
            rs_b(i)

    at_away(away_7)
    for i in first:
        rs_c(i)
    for i in last:
        rs_b(i)

    def home_7():
        trace_sum()
        for i in middle:
            rs_b(i)

    at_home(home_7)
    for i in middle:
        rs_c(i)
    for i in last:
        rs_c(i)

    def home_end():
        for i in range(nk):
            s, off, wc = chunks[i]
            local(10 + i, cbuf.at[cols(i)], out_panel.at[cols(i)]).wait()
            part = pl.ds(off, wc)
            local(26 + i, fsrc.at[s, :, part], out_sum.at[s, :, part]).wait()
        gone(st_v, "st")
        gone(dqd, "dqd")
        gone(dinv_r, "dinv")
        gone(tsum, "small")

    def away_end():
        gone(own_piece, "piece")
        gone(panel, "panel")
        gone(dq, "dq")
        gone(cbuf, "selected")
        gone(fsrc, "sums")
        gone(trs, "tile")
        got(out_panel, "selected")
        got(out_sum, "sums")

    gone(sig.at[pl.ds(0, 15)], "pieces")
    for i in range(nk):
        s, off, wc = chunks[i]
        gone(bs[i].at[pl.ds(0, 7)], "x", i)
        gone(ip.at[s, pl.ds(0, 7), :, pl.ds(off, wc)], "rs", i)
    gone(tra.at[pl.ds(0, 3)], "tiles")
    at_home(home_end)
    at_away(away_end)
    trace_got()


def write_kernel(p_in, diag_in, tr_in, p_out, diag_out, tr_out, tv, sem):
    ns = p_in.shape[0]
    copies = [
        pltpu.make_async_copy(src, dst, sem.at[i])
        for i, (src, dst) in enumerate(((tr_in, tv), (p_in, p_out), (diag_in, diag_out)))
    ]
    for copy in copies:
        copy.start()
    copies[0].wait()
    total = tv[0] + tv[1]
    for i in range(ns):
        tr_out[i] = jnp.sum(total[i : i + 1, :1])
    copies[1].wait()
    copies[2].wait()


def local(sigma_anc, panel, structure, d_inv, dq_panel, dq_diag):
    ns, w = panel.shape[0], panel.shape[2]
    share = w // 8
    chunks = chunks_of(ns, w)
    n_send, n_recv = all_slots(ns, len(chunks))[2:]
    bf, f32 = jnp.bfloat16, jnp.float32
    anywhere = pl.BlockSpec(memory_space=pl.ANY)
    hbm = pl.BlockSpec(memory_space=pltpu.HBM)
    smem = pl.BlockSpec(memory_space=pltpu.SMEM)
    found, sums, tr = pl.pallas_call(
        functools.partial(kernel, chunks),
        out_shape=(
            jax.ShapeDtypeStruct((ns, w, w), bf),
            jax.ShapeDtypeStruct((ns, share, w), f32),
            jax.ShapeDtypeStruct((2, 8, 128), f32),
        ),
        in_specs=[hbm] * 6,
        out_specs=(anywhere, anywhere, anywhere),
        scratch_shapes=[
            pltpu.VMEM((16, w, w // 2), bf),
            *[pltpu.VMEM((8, w, wc), bf) for _, _, wc in chunks],
            pltpu.VMEM((w, w), f32),
            pltpu.VMEM((ns, w, w), bf),
            pltpu.VMEM((ns, w, w), bf),
            pltpu.VMEM((ns, w, w), bf),
            pltpu.VMEM((ns, 8, share, w), f32),
            pltpu.VMEM((ns, 4, share, w), f32),
            pltpu.VMEM((ns, 4, share, w), f32),
            pltpu.VMEM((ns, 2, share // 2, w), f32),
            pltpu.VMEM((ns, 2, share, w), f32),
            pltpu.VMEM((ns, share, w), f32),
            pltpu.VMEM((ns, w, w), bf),
            pltpu.VMEM((ns, w, w), bf),
            pltpu.VMEM((ns, share, w), bf),
            pltpu.VMEM((ns, w, w), bf),
            pltpu.VMEM((8, 128), f32),
            pltpu.VMEM((8, 128), f32),
            pltpu.VMEM((8, 8, 128), f32),
            pltpu.VMEM((8, 128), f32),
            pltpu.VMEM((8, 128), jnp.int32),
            pltpu.SMEM((8, 128), jnp.int32),
            pltpu.SMEM(structure.shape, jnp.int32),
            pltpu.SemaphoreType.DMA((n_send,)),
            pltpu.SemaphoreType.DMA((n_recv,)),
            pltpu.SemaphoreType.DMA((32,)),
        ],
        compiler_params=pltpu.CompilerParams(
            collective_id=0, has_side_effects=True, vmem_limit_bytes=44 * 1024 * 1024
        ),
        name="selected_inverse",
    )(*(pltpu.with_memory_space_constraint(v, pltpu.HBM) for v in (structure, sigma_anc, panel, dq_panel, dq_diag, d_inv)))
    return pl.pallas_call(
        write_kernel,
        out_shape=(
            jax.ShapeDtypeStruct((ns, w, w), bf),
            jax.ShapeDtypeStruct((ns, share, w), f32),
            jax.ShapeDtypeStruct((ns,), f32),
        ),
        in_specs=[anywhere] * 3,
        out_specs=(hbm, hbm, smem),
        scratch_shapes=[
            pltpu.VMEM((2, 8, 128), f32),
            pltpu.SemaphoreType.DMA((3,)),
        ],
        compiler_params=pltpu.CompilerParams(vmem_limit_bytes=4 * 1024 * 1024),
        name="write_results",
    )(found, sums, tr)


def solution(mesh):
    return jax.shard_map(
        local,
        mesh=mesh,
        in_specs=(
            P("row", "col"),
            P("col", "row", None),
            P("col", None),
            P("col", None, None),
            P("col", "row", None),
            P("col", None, None),
        ),
        out_specs=(P("col", "row", None), P("col", "row", None), P("col")),
        check_vma=False,
    )
```

```python
import functools

import jax
import jax.numpy as jnp
from jax import lax
from jax.experimental import pallas as pl
from jax.experimental.pallas import tpu as pltpu
from jax.sharding import PartitionSpec as P

MESH = pl.DeviceIdType.MESH
PANEL, DQ, SEL = 0, 1, 2
SPLIT = (2, 2, 2)


def chunks_of(ns, w):
    out = []
    for i in range(ns):
        n = SPLIT[i % len(SPLIT)]
        out += [(i, j * (w // n), w // n) for j in range(n)]
    return out


class Slots:
    def __init__(self):
        self.at = {}

    def __call__(self, *name, span=1):
        if name not in self.at:
            self.at[name] = sum(self.size.values()) if hasattr(self, "size") else 0
            self.size = getattr(self, "size", {})
            self.size[name] = span
        return self.at[name]


def all_slots(ns, nk):
    send, recv = Slots(), Slots()
    for name in ("pieces", "piece", "panel", "dq", "selected", "sums", "tiles", "tile", "small", "st", "dqd", "dinv"):
        send(name)
    for i in range(nk):
        send("x", i)
        send("rs", i)
    for name in ("st", "dqd", "dinv", "az_own", "az_nb", "az_nb2", "az_far", "ayf", "selected", "sums", "tiles", "trz"):
        recv(name)
    for d in range(2):
        for j in range(2):
            recv("ay", d, j)
        for i in range(nk):
            recv("xo", d, i)
    for i in range(nk):
        for name in ("xf", "xs", "rs1", "rsa", "rsb", "panel"):
            recv(name, i)
    for i in range(ns):
        recv("dq", i)
    return send, recv, sum(send.size.values()), sum(recv.size.values())


def kernel(
    chunks, struct, sigma, panel, dq, dqd, dinv,
    out_panel, out_sum, out_tr,
    sig, *rest,
):
    nk = len(chunks)
    ns = chunks[-1][0] + 1
    bs = rest[:nk]
    (dqv, cbuf, own_t, ip, rk, sx, ra, rr, fsrc, dqd_v, dinv_v, dinv_r, own_v, td, trs, tra, tsum, st_v, st_s, st_in,
     send_sem, recv_sem, loc_sem, ready, turn) = rest[nk + 1 :]
    prod = rest[nk]
    w = dqv.shape[1]
    hw = w // 2
    share = w // 8
    send_at, recv_at = all_slots(ns, nk)[:2]

    row, col = lax.axis_index("row"), lax.axis_index("col")
    x, zh = row // 2, row % 2
    y, zl, c = col // 4, (col // 2) % 2, col % 2
    z = zh * 2 + zl
    home = c == zh
    hb = 1 - (c + zh) % 2
    up = (hb + zl) % 2
    r = 2 * x + c
    xp, xm, xq = (x + 1) % 4, (x + 3) % 4, (x + 2) % 4
    yp, ym, yq = (y + 1) % 4, (y + 3) % 4, (y + 2) % 4
    zp, zm, zq = (z + 1) % 4, (z + 3) % 4, (z + 2) % 4

    def dev(x_, y_, z_, c_):
        return (x_ * 2 + z_ // 2, (y_ * 2 + z_ % 2) * 2 + c_)

    sib = dev(x, y, z, 1 - c)
    partner = dev(x, y, zq, 1 - c)


    def go(src, dst, sname, rname, to):
        pltpu.make_async_remote_copy(
            src_ref=src,
            dst_ref=dst,
            send_sem=send_sem.at[send_at(*sname)],
            recv_sem=recv_sem.at[recv_at(*rname)],
            device_id=to,
            device_id_type=MESH,
        ).start()

    def got(dst, *name):
        pltpu.make_async_copy(dst, dst, recv_sem.at[recv_at(*name)]).wait()

    def gone(src, *name):
        pltpu.make_async_copy(src, src, send_sem.at[send_at(*name)]).wait()

    def local(i, src, dst):
        return pltpu.make_async_copy(src, dst, loc_sem.at[i])

    def at_home(f):
        pl.when(home)(f)

    def at_away(f):
        pl.when(jnp.logical_not(home))(f)

    own_piece = sig.at[4 * y + 2 * zl + c]

    def az_send():
        for d in range(2):
            for z_, h in ((zp, d), (zm, 1 - d)):
                rows = pl.ds(h * hw, hw)
                go(sigma.at[rows], sig.at[4 * y + 2 * zl + c, rows], ("pieces",), (("az_nb", "az_nb2")[d],),
                   dev(x, y, z_, zh))

    def az_own_away():
        go(sigma, own_piece, ("piece",), ("az_own",), sib)

    def az_near():
        part = sig.at[pl.ds(4 * y + 2 * (1 - zl), 2), pl.ds(pl.multiple_of(up * hw, hw), hw)]
        got(part, "az_nb")
        go(part, part, ("pieces",), ("az_far",), dev(x, y, (z + 1 + 2 * up) % 4, c))
        got(part, "az_nb2")

    def az_far():
        got(sig.at[pl.ds(4 * y + 2 * zl, 2)], "az_far")

    pair_zl = ((zl * hb + (1 - zl) * (1 - hb)), ((1 - zl) * hb + zl * (1 - hb)))

    def pair(y_, j):
        return sig.at[pl.ds(4 * y_ + 2 * pair_zl[j], 2)]

    def ay_send(j):
        go(pair(y, j), pair(y, j), ("pieces",), ("ay", 0, j), dev(x, yp, z, c))
        go(pair(y, j), pair(y, j), ("pieces",), ("ay", 1, j), dev(x, ym, z, c))

    def ay_forward(j):
        got(pair(ym, j), "ay", 0, j)
        p0 = sig.at[4 * ym + 2 * pair_zl[j]]
        go(p0, p0, ("pieces",), ("ayf",), dev(x, yp, z, c))
        got(pair(yp, j), "ay", 1, j)
        p1 = sig.at[4 * yp + 2 * pair_zl[j] + 1]
        go(p1, p1, ("pieces",), ("ayf",), dev(x, ym, z, c))

    def ay_done():
        got(sig.at[pl.ds(4 * yq, 4)], "ayf")

    def blk(i, x_, c_=None):
        return bs[i].at[2 * x_ + (c if c_ is None else c_)]

    def half(i, x_, d):
        return bs[i].at[2 * x_ + c, pl.ds(d * hw, hw)]

    def to_sib(i, x_):
        go(blk(i, x_), blk(i, x_), ("x", i), ("xs", i), sib)

    def x_own(i):
        go(blk(i, x), blk(i, x), ("x", i), ("xo", 0, i), dev(xp, y, z, c))
        go(blk(i, x), blk(i, x), ("x", i), ("xo", 1, i), dev(xm, y, z, c))
        to_sib(i, x)

    def x_forward(i):
        got(blk(i, xm), "xo", 0, i)
        go(half(i, xm, 0), half(i, xm, 0), ("x", i), ("xf", i), dev(xp, y, z, c))
        got(blk(i, xp), "xo", 1, i)
        go(half(i, xp, 1), half(i, xp, 1), ("x", i), ("xf", i), dev(xm, y, z, c))
        to_sib(i, xm)
        to_sib(i, xp)

    def x_far(i):
        got(blk(i, xq), "xf", i)
        to_sib(i, xq)

    def x_sib(i):
        got(bs[i].at[pl.ds(0, 4)], "xs", i)

    def cols(i):
        return chunks[i][0], slice(None), pl.ds(chunks[i][1], chunks[i][2])

    def sw_dst(kind, i, r_):
        if kind == PANEL:
            return bs[i].at[r_]
        return dqv.at[i] if kind == DQ else out_panel.at[cols(i)]

    def sw_send(kind, i):
        src = panel.at[cols(i)] if kind == PANEL else dq.at[i] if kind == DQ else cbuf.at[cols(i)]
        name = ("panel", "dq", "selected")[kind]
        go(src, sw_dst(kind, i, 2 * x + 1 - c), (name,), (name,) if kind == SEL else (name, i), partner)

    def sw_got(kind, i):
        got(sw_dst(kind, i, r), ("panel", "dq")[kind], i)

    def turn_own():
        for i, (s, off, wc) in enumerate(chunks):
            own_t[s, off : off + wc, :] = bs[i][r].T

    def compute(i):
        b = bs[i]
        s, off, wc = chunks[i]
        lanes = slice(off, off + wc)

        def step(t, carry):
            k = st_s[s, t]
            v = jnp.dot(sig[2 * k], b[k, :hw], preferred_element_type=jnp.float32)
            v += jnp.dot(sig[2 * k + 1], b[k, hw:], preferred_element_type=jnp.float32)
            prod[:, :wc] += v
            return carry

        prod[:, :wc] = jnp.zeros((w, wc), jnp.float32)
        lax.fori_loop(0, 4, step, 0)
        here = jnp.float32(0)
        for t in range(4):
            here += jnp.where(st_s[s, t] == r, jnp.float32(1), jnp.float32(0))
        kept = prod[:, :wc] * here
        hi = kept.astype(jnp.bfloat16)
        cbuf[s, :, lanes] = -hi

        def selected_home():
            local(10 + i, cbuf.at[cols(i)], out_panel.at[cols(i)]).start()

        at_home(selected_home)
        at_away(lambda: sw_send(SEL, i))
        lo = (kept - hi.astype(jnp.float32)).astype(jnp.bfloat16)
        trace = -2.0 * jnp.sum(kept * dqv[s, :, lanes].astype(jnp.float32), axis=0, keepdims=True)
        inner = jnp.dot(own_t[s], hi, preferred_element_type=jnp.float32)
        inner += jnp.dot(own_t[s], lo, preferred_element_type=jnp.float32)
        for a in range(8):
            ip[s, 4 * (a % 2) + a // 2, :, lanes] = inner[a * share : (a + 1) * share]
        trace += jnp.sum(inner * dqd_v[s, :, lanes].astype(jnp.float32), axis=0, keepdims=True)
        part = pl.ds(off, wc)
        go(ip.at[s, pl.ds(4 * (1 - c), 4), :, part], rk.at[s, :, :, part], ("rs", i), ("rs1", i), sib)
        trs[s : s + 1, :] += jnp.broadcast_to(jnp.sum(trace, axis=1, keepdims=True), (1, 128))

    hs = share // 2
    near = (xp, xm)

    def rs_a(i):
        s, off, wc = chunks[i]
        lanes, part = slice(off, off + wc), pl.ds(off, wc)
        got(rk.at[s, :, :, part], "rs1", i)
        sx[s, :, :, lanes] = ip[s, pl.ds(4 * c, 4), :, lanes] + rk[s, :, :, lanes]
        for d in range(2):
            go(sx.at[s, xq, pl.ds(d * hs, hs), part], ra.at[s, d, :, part], ("rs", i), ("rsa", i),
               dev(near[d], y, z, c))

    def rs_b(i):
        s, off, wc = chunks[i]
        lanes, part = slice(off, off + wc), pl.ds(off, wc)
        got(ra.at[s, :, :, part], "rsa", i)
        for d in range(2):
            sx[s, near[d], d * hs : (d + 1) * hs, lanes] += ra[s, d, :, lanes]
            go(sx.at[s, near[d], :, part], rr.at[s, d, :, part], ("rs", i), ("rsb", i), dev(near[d], y, z, c))

    def rs_c(i):
        s, off, wc = chunks[i]
        lanes, part = slice(off, off + wc), pl.ds(off, wc)
        got(rr.at[s, :, :, part], "rsb", i)
        total = sx[s, x, :, lanes] + rr[s, 0, :, lanes] + rr[s, 1, :, lanes]
        fsrc[s, :, lanes] = dinv_r[s, :, lanes].astype(jnp.float32) + total

        at_home(lambda: local(26 + i, fsrc.at[s, :, part], out_sum.at[s, :, part]).start())
        at_away(lambda: go(fsrc.at[s, :, part], out_sum.at[s, :, part], ("sums",), ("sums",), partner))

    def own_trace():
        local(4, dinv, dinv_v).wait()
        local(5, dqd, own_v).wait()
        td[...] = jnp.zeros_like(td)
        for i in range(ns):
            v = jnp.sum(dinv_v[i].astype(jnp.float32) * own_v[i].astype(jnp.float32), axis=0, keepdims=True)
            td[i : i + 1, :] = jnp.broadcast_to(jnp.sum(v, axis=1, keepdims=True), (1, 128))
        local(6, td, out_tr.at[1]).start()

    def trace_send():
        def tile(dx, name):
            go(trs, tra.at[2 * dx + c], (name,), ("tiles",), dev((x + dx) % 4, y, z, zh))

        at_away(lambda: tile(0, "tile"))
        at_home(keep_tile)
        for dx in range(1, 4):
            tile(dx, "tiles")

    def keep_tile():
        tsum[...] = trs[...]

    def trace_sum():
        got(tra.at[pl.ds(0, 7)], "tiles")
        total = tsum[...]
        for k in range(2, 8):
            total += tra[k]
        tsum[...] = total + tra[1 - c]
        local(8, tsum, out_tr.at[0]).start()
        go(tsum, out_tr.at[0], ("small",), ("trz",), dev(x, y, zq, c))

    def trace_got():
        local(6, td, out_tr.at[1]).wait()
        at_home(lambda: local(8, tsum, out_tr.at[0]).wait())
        at_away(lambda: got(out_tr.at[0], "trz"))

    barrier = pltpu.get_barrier_semaphore()
    peers = [dev(x, yp, z, c), dev(x, ym, z, c), sib]
    for c_ in (0, 1):
        peers += [dev(x_, y, z, c_) for x_ in (xp, xm, xq)]
        peers += [dev(x, y, z_, c_) for z_ in (zp, zm, zq)]
    for peer in peers:
        pl.semaphore_signal(barrier, inc=1, device_id=peer, device_id_type=MESH)

    at_home(lambda: [local(20 + i, panel.at[cols(i)], bs[i].at[r]).start() for i in range(nk)] and None)
    at_home(lambda: local(0, sigma, own_piece).start())
    at_home(lambda: local(7, struct, st_in).start())

    def structure_out():
        rows = lax.broadcasted_iota(jnp.int32, st_v.shape, 0)
        lanes = lax.broadcasted_iota(jnp.int32, st_v.shape, 1)
        local(7, struct, st_in).wait()
        v = jnp.zeros(st_v.shape, jnp.int32)
        for i in range(ns):
            for t in range(4):
                v = jnp.where((rows == i) & (lanes == t), st_in[i, t], v)
        st_v[...] = v

    at_home(structure_out)
    pl.semaphore_wait(barrier, len(peers))

    az_send()
    at_away(az_own_away)
    at_home(lambda: go(st_v, st_v, ("st",), ("st",), sib))
    last = [i for i in range(nk) if chunks[i][0] == ns - 1]
    early = [i for i in range(nk) if i not in last]
    first = [i for i in early if chunks[i][0] == 0]
    middle = [i for i in early if i not in first]

    def own_from_home(i):
        local(20 + i, panel.at[cols(i)], bs[i].at[r]).wait()
        x_own(i)

    def d_rows(r_):
        return dinv.at[:, pl.ds(pl.multiple_of(r_ * share, share), share)]

    def home_start():
        for i in early:
            own_from_home(i)
        local(0, sigma, own_piece).wait()
        got(own_piece, "az_own")
        ay_send(0)
        local(1, dq, dqv).start()
        local(2, dqd, dqd_v).start()
        go(dqd, dqd_v, ("dqd",), ("dqd",), sib)
        local(9, d_rows(r), dinv_r).start()
        go(d_rows(2 * x + 1 - c), dinv_r, ("dinv",), ("dinv",), sib)

    at_home(home_start)
    local(4, dinv, dinv_v).start()
    local(5, dqd, own_v).start()
    az_near()

    def home_1():
        ay_send(1)
        for i in first:
            x_forward(i)

    def own_from_away(i):
        sw_got(PANEL, i)
        x_own(i)

    def away_1():
        ay_send(0)
        az_far()
        pl.semaphore_signal(ready, inc=1, device_id=partner, device_id_type=MESH)
        ay_send(1)
        pl.semaphore_wait(ready, 1)
        for i in range(nk):
            sw_send(PANEL, i)
        for i in range(ns):
            sw_send(DQ, i)
        for i in first:
            own_from_away(i)

    at_home(home_1)
    at_away(away_1)
    ay_forward(0)

    def home_2():
        for i in middle:
            x_forward(i)
        for i in last:
            own_from_home(i)
        for i in first:
            x_far(i)

    def away_2():
        for i in middle:
            own_from_away(i)
        for i in first:
            x_forward(i)

    at_home(home_2)
    at_away(away_2)
    ay_forward(1)

    def home_3():
        for i in middle:
            x_far(i)
        turn_own()
        local(1, dq, dqv).wait()
        local(2, dqd, dqd_v).wait()
        local(9, d_rows(r), dinv_r).wait()
        for i in last:
            x_forward(i)
        for i in last:
            x_far(i)

    def away_3():
        for i in last:
            own_from_away(i)
        turn_own()
        for i in middle:
            x_forward(i)
        got(dqd_v, "dqd")
        got(dinv_r, "dinv")
        got(st_v, "st")
        for i in first:
            x_far(i)
        sw_got(DQ, 0)

    at_home(home_3)
    at_away(away_3)
    own_trace()
    cp = local(3, st_v, st_s)
    cp.start()
    cp.wait()
    trs[...] = jnp.zeros_like(trs)
    ay_done()
    ahead = list(last)
    for i in first:
        x_sib(i)
        compute(i)
        if ahead:
            at_away(lambda: x_forward(ahead[0]))
            ahead.pop(0)
    for i in ahead:
        at_away(lambda i=i: x_forward(i))
    for i in first:
        rs_a(i)

    def away_4():
        for i in range(1, ns - 1):
            sw_got(DQ, i)

    at_away(away_4)
    for i in middle:
        at_away(lambda i=i: x_far(i))
        x_sib(i)
        compute(i)
    def home_5():
        for i in middle:
            rs_a(i)

    def away_5():
        x_far(last[0])
        for i in first:
            rs_b(i)
        for i in last[1:]:
            x_far(i)
        sw_got(DQ, ns - 1)

    at_home(home_5)
    at_away(away_5)
    x_sib(last[0])
    compute(last[0])

    def away_6():
        for i in middle:
            rs_a(i)

    at_away(away_6)
    for i in last[1:]:
        x_sib(i)
        compute(i)
    trace_send()

    for i in last:
        rs_a(i)

    def away_7():
        for i in middle:
            rs_b(i)
        for i in first:
            rs_c(i)

    at_away(away_7)

    def home_turn():
        trace_sum()
        pl.semaphore_wait(turn, 1)
        for i in first:
            rs_b(i)

    at_home(home_turn)
    for i in last:
        rs_b(i)
    at_away(lambda: pl.semaphore_signal(turn, inc=1, device_id=sib, device_id_type=MESH))

    def home_7():
        for i in middle:
            rs_b(i)
        for i in first:
            rs_c(i)

    at_home(home_7)
    for i in middle:
        rs_c(i)
    for i in last:
        rs_c(i)

    def home_end():
        for i in range(nk):
            s, off, wc = chunks[i]
            local(10 + i, cbuf.at[cols(i)], out_panel.at[cols(i)]).wait()
            part = pl.ds(off, wc)
            local(26 + i, fsrc.at[s, :, part], out_sum.at[s, :, part]).wait()
        gone(st_v, "st")
        gone(dqd, "dqd")
        gone(dinv_r, "dinv")
        gone(tsum, "small")

    def away_end():
        gone(own_piece, "piece")
        gone(panel, "panel")
        gone(dq, "dq")
        gone(cbuf, "selected")
        gone(fsrc, "sums")
        gone(trs, "tile")
        got(out_panel, "selected")
        got(out_sum, "sums")

    gone(sig.at[pl.ds(0, 15)], "pieces")
    for i in range(nk):
        s, off, wc = chunks[i]
        gone(bs[i].at[pl.ds(0, 7)], "x", i)
        gone(ip.at[s, pl.ds(0, 7), :, pl.ds(off, wc)], "rs", i)
    gone(tra.at[pl.ds(0, 3)], "tiles")
    at_home(home_end)
    at_away(away_end)
    trace_got()


def write_kernel(p_in, diag_in, tr_in, p_out, diag_out, tr_out, tv, sem):
    ns = p_in.shape[0]
    copies = [
        pltpu.make_async_copy(src, dst, sem.at[i])
        for i, (src, dst) in enumerate(((tr_in, tv), (p_in, p_out), (diag_in, diag_out)))
    ]
    for copy in copies:
        copy.start()
    copies[0].wait()
    total = tv[0] + tv[1]
    for i in range(ns):
        tr_out[i] = jnp.sum(total[i : i + 1, :1])
    copies[1].wait()
    copies[2].wait()


def local(sigma_anc, panel, structure, d_inv, dq_panel, dq_diag):
    ns, w = panel.shape[0], panel.shape[2]
    share = w // 8
    chunks = chunks_of(ns, w)
    n_send, n_recv = all_slots(ns, len(chunks))[2:]
    bf, f32 = jnp.bfloat16, jnp.float32
    anywhere = pl.BlockSpec(memory_space=pl.ANY)
    hbm = pl.BlockSpec(memory_space=pltpu.HBM)
    smem = pl.BlockSpec(memory_space=pltpu.SMEM)
    found, sums, tr = pl.pallas_call(
        functools.partial(kernel, chunks),
        out_shape=(
            jax.ShapeDtypeStruct((ns, w, w), bf),
            jax.ShapeDtypeStruct((ns, share, w), f32),
            jax.ShapeDtypeStruct((2, 8, 128), f32),
        ),
        in_specs=[hbm] * 6,
        out_specs=(anywhere, anywhere, anywhere),
        scratch_shapes=[
            pltpu.VMEM((16, w, w // 2), bf),
            *[pltpu.VMEM((8, w, wc), bf) for _, _, wc in chunks],
            pltpu.VMEM((w, w), f32),
            pltpu.VMEM((ns, w, w), bf),
            pltpu.VMEM((ns, w, w), bf),
            pltpu.VMEM((ns, w, w), bf),
            pltpu.VMEM((ns, 8, share, w), f32),
            pltpu.VMEM((ns, 4, share, w), f32),
            pltpu.VMEM((ns, 4, share, w), f32),
            pltpu.VMEM((ns, 2, share // 2, w), f32),
            pltpu.VMEM((ns, 2, share, w), f32),
            pltpu.VMEM((ns, share, w), f32),
            pltpu.VMEM((ns, w, w), bf),
            pltpu.VMEM((ns, w, w), bf),
            pltpu.VMEM((ns, share, w), bf),
            pltpu.VMEM((ns, w, w), bf),
            pltpu.VMEM((8, 128), f32),
            pltpu.VMEM((8, 128), f32),
            pltpu.VMEM((8, 8, 128), f32),
            pltpu.VMEM((8, 128), f32),
            pltpu.VMEM((8, 128), jnp.int32),
            pltpu.SMEM((8, 128), jnp.int32),
            pltpu.SMEM(structure.shape, jnp.int32),
            pltpu.SemaphoreType.DMA((n_send,)),
            pltpu.SemaphoreType.DMA((n_recv,)),
            pltpu.SemaphoreType.DMA((32,)),
            pltpu.SemaphoreType.REGULAR,
            pltpu.SemaphoreType.REGULAR,
        ],
        compiler_params=pltpu.CompilerParams(
            collective_id=0, has_side_effects=True, vmem_limit_bytes=44 * 1024 * 1024
        ),
        name="selected_inverse",
    )(*(pltpu.with_memory_space_constraint(v, pltpu.HBM) for v in (structure, sigma_anc, panel, dq_panel, dq_diag, d_inv)))
    return pl.pallas_call(
        write_kernel,
        out_shape=(
            jax.ShapeDtypeStruct((ns, w, w), bf),
            jax.ShapeDtypeStruct((ns, share, w), f32),
            jax.ShapeDtypeStruct((ns,), f32),
        ),
        in_specs=[anywhere] * 3,
        out_specs=(hbm, hbm, smem),
        scratch_shapes=[
            pltpu.VMEM((2, 8, 128), f32),
            pltpu.SemaphoreType.DMA((3,)),
        ],
        compiler_params=pltpu.CompilerParams(vmem_limit_bytes=4 * 1024 * 1024),
        name="write_results",
    )(found, sums, tr)


def solution(mesh):
    return jax.shard_map(
        local,
        mesh=mesh,
        in_specs=(
            P("row", "col"),
            P("col", "row", None),
            P("col", None),
            P("col", None, None),
            P("col", "row", None),
            P("col", None, None),
        ),
        out_specs=(P("col", "row", None), P("col", "row", None), P("col")),
        check_vma=False,
    )
```

```python
import functools

import jax
import jax.numpy as jnp
from jax import lax
from jax.experimental import pallas as pl
from jax.experimental.pallas import tpu as pltpu
from jax.sharding import PartitionSpec as P

MESH = pl.DeviceIdType.MESH
PANEL, DQ, SEL = 0, 1, 2
SPLIT = (2, 2, 2)


def chunks_of(ns, w):
    out = []
    for i in range(ns):
        n = SPLIT[i % len(SPLIT)]
        out += [(i, j * (w // n), w // n) for j in range(n)]
    return out


class Slots:
    def __init__(self):
        self.at = {}

    def __call__(self, *name, span=1):
        if name not in self.at:
            self.at[name] = sum(self.size.values()) if hasattr(self, "size") else 0
            self.size = getattr(self, "size", {})
            self.size[name] = span
        return self.at[name]


def all_slots(ns, nk):
    send, recv = Slots(), Slots()
    for name in ("pieces", "piece", "panel", "dq", "selected", "sums", "tiles", "tile", "small", "st", "dqd", "dinv"):
        send(name)
    for i in range(nk):
        send("x", i)
        send("rs", i)
    for name in ("st", "dqd", "dinv", "az_own", "az_nb", "az_nb2", "az_far", "ayf", "selected", "sums", "tiles", "trz"):
        recv(name)
    for d in range(2):
        for j in range(2):
            recv("ay", d, j)
        for i in range(nk):
            recv("xo", d, i)
    for i in range(nk):
        for name in ("xf", "xs", "rs1", "rsa", "rsb", "panel"):
            recv(name, i)
    for i in range(ns):
        recv("dq", i)
    return send, recv, sum(send.size.values()), sum(recv.size.values())


def kernel(
    chunks, struct, sigma, panel, dq, dqd, dinv,
    out_panel, out_sum, out_tr,
    sig, *rest,
):
    nk = len(chunks)
    ns = chunks[-1][0] + 1
    bs = rest[:nk]
    (dqv, cbuf, own_t, ip, rk, sx, ra, rr, fsrc, dqd_v, dinv_v, dinv_r, own_v, td, trs, tra, tsum, st_v, st_s, st_in,
     send_sem, recv_sem, loc_sem, ready, turn) = rest[nk + 1 :]
    prod = rest[nk]
    w = dqv.shape[1]
    hw = w // 2
    share = w // 8
    send_at, recv_at = all_slots(ns, nk)[:2]

    row, col = lax.axis_index("row"), lax.axis_index("col")
    x, zh = row // 2, row % 2
    y, zl, c = col // 4, (col // 2) % 2, col % 2
    z = zh * 2 + zl
    home = c == zh
    hb = 1 - (c + zh) % 2
    up = (hb + zl) % 2
    r = 2 * x + c
    xp, xm, xq = (x + 1) % 4, (x + 3) % 4, (x + 2) % 4
    yp, ym, yq = (y + 1) % 4, (y + 3) % 4, (y + 2) % 4
    zp, zm, zq = (z + 1) % 4, (z + 3) % 4, (z + 2) % 4

    def dev(x_, y_, z_, c_):
        return (x_ * 2 + z_ // 2, (y_ * 2 + z_ % 2) * 2 + c_)

    sib = dev(x, y, z, 1 - c)
    partner = dev(x, y, zq, 1 - c)


    def go(src, dst, sname, rname, to):
        pltpu.make_async_remote_copy(
            src_ref=src,
            dst_ref=dst,
            send_sem=send_sem.at[send_at(*sname)],
            recv_sem=recv_sem.at[recv_at(*rname)],
            device_id=to,
            device_id_type=MESH,
        ).start()

    def got(dst, *name):
        pltpu.make_async_copy(dst, dst, recv_sem.at[recv_at(*name)]).wait()

    def gone(src, *name):
        pltpu.make_async_copy(src, src, send_sem.at[send_at(*name)]).wait()

    def local(i, src, dst):
        return pltpu.make_async_copy(src, dst, loc_sem.at[i])

    def at_home(f):
        pl.when(home)(f)

    def at_away(f):
        pl.when(jnp.logical_not(home))(f)

    own_piece = sig.at[4 * y + 2 * zl + c]

    def az_send():
        for d in range(2):
            for z_, h in ((zp, d), (zm, 1 - d)):
                rows = pl.ds(h * hw, hw)
                go(sigma.at[rows], sig.at[4 * y + 2 * zl + c, rows], ("pieces",), (("az_nb", "az_nb2")[d],),
                   dev(x, y, z_, zh))

    def az_own_away():
        go(sigma, own_piece, ("piece",), ("az_own",), sib)

    def az_near():
        part = sig.at[pl.ds(4 * y + 2 * (1 - zl), 2), pl.ds(pl.multiple_of(up * hw, hw), hw)]
        got(part, "az_nb")
        go(part, part, ("pieces",), ("az_far",), dev(x, y, (z + 1 + 2 * up) % 4, c))
        got(part, "az_nb2")

    def az_far():
        got(sig.at[pl.ds(4 * y + 2 * zl, 2)], "az_far")

    pair_zl = ((zl * hb + (1 - zl) * (1 - hb)), ((1 - zl) * hb + zl * (1 - hb)))

    def pair(y_, j):
        return sig.at[pl.ds(4 * y_ + 2 * pair_zl[j], 2)]

    def ay_send(j):
        go(pair(y, j), pair(y, j), ("pieces",), ("ay", 0, j), dev(x, yp, z, c))
        go(pair(y, j), pair(y, j), ("pieces",), ("ay", 1, j), dev(x, ym, z, c))

    def ay_forward(j):
        got(pair(ym, j), "ay", 0, j)
        p0 = sig.at[4 * ym + 2 * pair_zl[j]]
        go(p0, p0, ("pieces",), ("ayf",), dev(x, yp, z, c))
        got(pair(yp, j), "ay", 1, j)
        p1 = sig.at[4 * yp + 2 * pair_zl[j] + 1]
        go(p1, p1, ("pieces",), ("ayf",), dev(x, ym, z, c))

    def ay_done():
        got(sig.at[pl.ds(4 * yq, 4)], "ayf")

    def blk(i, x_, c_=None):
        return bs[i].at[2 * x_ + (c if c_ is None else c_)]

    def half(i, x_, d):
        return bs[i].at[2 * x_ + c, pl.ds(d * hw, hw)]

    def to_sib(i, x_):
        go(blk(i, x_), blk(i, x_), ("x", i), ("xs", i), sib)

    def x_own(i):
        go(blk(i, x), blk(i, x), ("x", i), ("xo", 0, i), dev(xp, y, z, c))
        go(blk(i, x), blk(i, x), ("x", i), ("xo", 1, i), dev(xm, y, z, c))
        to_sib(i, x)

    def x_forward(i):
        got(blk(i, xm), "xo", 0, i)
        go(half(i, xm, 0), half(i, xm, 0), ("x", i), ("xf", i), dev(xp, y, z, c))
        got(blk(i, xp), "xo", 1, i)
        go(half(i, xp, 1), half(i, xp, 1), ("x", i), ("xf", i), dev(xm, y, z, c))
        to_sib(i, xm)
        to_sib(i, xp)

    def x_far(i):
        got(blk(i, xq), "xf", i)
        to_sib(i, xq)

    def x_sib(i):
        got(bs[i].at[pl.ds(0, 4)], "xs", i)

    def cols(i):
        return chunks[i][0], slice(None), pl.ds(chunks[i][1], chunks[i][2])

    def sw_dst(kind, i, r_):
        if kind == PANEL:
            return bs[i].at[r_]
        return dqv.at[i] if kind == DQ else out_panel.at[cols(i)]

    def sw_send(kind, i):
        src = panel.at[cols(i)] if kind == PANEL else dq.at[i] if kind == DQ else cbuf.at[cols(i)]
        name = ("panel", "dq", "selected")[kind]
        go(src, sw_dst(kind, i, 2 * x + 1 - c), (name,), (name,) if kind == SEL else (name, i), partner)

    def sw_got(kind, i):
        got(sw_dst(kind, i, r), ("panel", "dq")[kind], i)

    def turn_own():
        for i, (s, off, wc) in enumerate(chunks):
            own_t[s, off : off + wc, :] = bs[i][r].T

    def compute(i):
        b = bs[i]
        s, off, wc = chunks[i]
        lanes = slice(off, off + wc)

        def step(t, carry):
            k = st_s[s, t]
            v = jnp.dot(sig[2 * k], b[k, :hw], preferred_element_type=jnp.float32)
            v += jnp.dot(sig[2 * k + 1], b[k, hw:], preferred_element_type=jnp.float32)
            prod[:, :wc] += v
            return carry

        prod[:, :wc] = jnp.zeros((w, wc), jnp.float32)
        lax.fori_loop(0, 4, step, 0)
        here = jnp.float32(0)
        for t in range(4):
            here += jnp.where(st_s[s, t] == r, jnp.float32(1), jnp.float32(0))
        kept = prod[:, :wc] * here
        hi = kept.astype(jnp.bfloat16)
        cbuf[s, :, lanes] = -hi

        def selected_home():
            local(10 + i, cbuf.at[cols(i)], out_panel.at[cols(i)]).start()

        at_home(selected_home)
        at_away(lambda: sw_send(SEL, i))
        lo = (kept - hi.astype(jnp.float32)).astype(jnp.bfloat16)
        trace = -2.0 * jnp.sum(kept * dqv[s, :, lanes].astype(jnp.float32), axis=0, keepdims=True)
        inner = jnp.dot(own_t[s], hi, preferred_element_type=jnp.float32)
        inner += jnp.dot(own_t[s], lo, preferred_element_type=jnp.float32)
        for a in range(8):
            ip[s, 4 * (a % 2) + a // 2, :, lanes] = inner[a * share : (a + 1) * share]
        trace += jnp.sum(inner * dqd_v[s, :, lanes].astype(jnp.float32), axis=0, keepdims=True)
        part = pl.ds(off, wc)
        go(ip.at[s, pl.ds(4 * (1 - c), 4), :, part], rk.at[s, :, :, part], ("rs", i), ("rs1", i), sib)
        trs[s : s + 1, :] += jnp.broadcast_to(jnp.sum(trace, axis=1, keepdims=True), (1, 128))

    hs = share // 2
    near = (xp, xm)

    def rs_a(i):
        s, off, wc = chunks[i]
        lanes, part = slice(off, off + wc), pl.ds(off, wc)
        got(rk.at[s, :, :, part], "rs1", i)
        sx[s, :, :, lanes] = ip[s, pl.ds(4 * c, 4), :, lanes] + rk[s, :, :, lanes]
        for d in range(2):
            go(sx.at[s, xq, pl.ds(d * hs, hs), part], ra.at[s, d, :, part], ("rs", i), ("rsa", i),
               dev(near[d], y, z, c))

    def rs_b(i):
        s, off, wc = chunks[i]
        lanes, part = slice(off, off + wc), pl.ds(off, wc)
        got(ra.at[s, :, :, part], "rsa", i)
        for d in range(2):
            sx[s, near[d], d * hs : (d + 1) * hs, lanes] += ra[s, d, :, lanes]
            go(sx.at[s, near[d], :, part], rr.at[s, d, :, part], ("rs", i), ("rsb", i), dev(near[d], y, z, c))

    def rs_c(i):
        s, off, wc = chunks[i]
        lanes, part = slice(off, off + wc), pl.ds(off, wc)
        got(rr.at[s, :, :, part], "rsb", i)
        total = sx[s, x, :, lanes] + rr[s, 0, :, lanes] + rr[s, 1, :, lanes]
        fsrc[s, :, lanes] = dinv_r[s, :, lanes].astype(jnp.float32) + total

        at_home(lambda: local(26 + i, fsrc.at[s, :, part], out_sum.at[s, :, part]).start())
        at_away(lambda: go(fsrc.at[s, :, part], out_sum.at[s, :, part], ("sums",), ("sums",), partner))

    def own_trace():
        local(4, dinv, dinv_v).wait()
        local(5, dqd, own_v).wait()
        td[...] = jnp.zeros_like(td)
        for i in range(ns):
            v = jnp.sum(dinv_v[i].astype(jnp.float32) * own_v[i].astype(jnp.float32), axis=0, keepdims=True)
            td[i : i + 1, :] = jnp.broadcast_to(jnp.sum(v, axis=1, keepdims=True), (1, 128))
        local(6, td, out_tr.at[1]).start()

    def trace_send():
        def tile(dx, name):
            go(trs, tra.at[2 * dx + c], (name,), ("tiles",), dev((x + dx) % 4, y, z, zh))

        at_away(lambda: tile(0, "tile"))
        at_home(keep_tile)
        for dx in range(1, 4):
            tile(dx, "tiles")

    def keep_tile():
        tsum[...] = trs[...]

    def trace_sum():
        got(tra.at[pl.ds(0, 7)], "tiles")
        total = tsum[...]
        for k in range(2, 8):
            total += tra[k]
        tsum[...] = total + tra[1 - c]
        local(8, tsum, out_tr.at[0]).start()
        go(tsum, out_tr.at[0], ("small",), ("trz",), dev(x, y, zq, c))

    def trace_got():
        local(6, td, out_tr.at[1]).wait()
        at_home(lambda: local(8, tsum, out_tr.at[0]).wait())
        at_away(lambda: got(out_tr.at[0], "trz"))

    barrier = pltpu.get_barrier_semaphore()
    peers = [dev(x, yp, z, c), dev(x, ym, z, c), sib]
    for c_ in (0, 1):
        peers += [dev(x_, y, z, c_) for x_ in (xp, xm, xq)]
        peers += [dev(x, y, z_, c_) for z_ in (zp, zm, zq)]
    for peer in peers:
        pl.semaphore_signal(barrier, inc=1, device_id=peer, device_id_type=MESH)

    at_home(lambda: [local(20 + i, panel.at[cols(i)], bs[i].at[r]).start() for i in range(nk)] and None)
    at_home(lambda: local(0, sigma, own_piece).start())
    at_home(lambda: local(7, struct, st_in).start())

    def structure_out():
        rows = lax.broadcasted_iota(jnp.int32, st_v.shape, 0)
        lanes = lax.broadcasted_iota(jnp.int32, st_v.shape, 1)
        local(7, struct, st_in).wait()
        v = jnp.zeros(st_v.shape, jnp.int32)
        for i in range(ns):
            for t in range(4):
                v = jnp.where((rows == i) & (lanes == t), st_in[i, t], v)
        st_v[...] = v

    at_home(structure_out)
    pl.semaphore_wait(barrier, len(peers))

    az_send()
    at_away(az_own_away)
    at_home(lambda: go(st_v, st_v, ("st",), ("st",), sib))
    last = [i for i in range(nk) if chunks[i][0] == ns - 1]
    early = [i for i in range(nk) if i not in last]
    first = [i for i in early if chunks[i][0] == 0]
    middle = [i for i in early if i not in first]

    def own_from_home(i):
        local(20 + i, panel.at[cols(i)], bs[i].at[r]).wait()
        x_own(i)

    def d_rows(r_):
        return dinv.at[:, pl.ds(pl.multiple_of(r_ * share, share), share)]

    def home_start():
        for i in early:
            own_from_home(i)
        local(0, sigma, own_piece).wait()
        got(own_piece, "az_own")
        ay_send(0)
        local(1, dq, dqv).start()
        local(2, dqd, dqd_v).start()
        go(dqd, dqd_v, ("dqd",), ("dqd",), sib)
        local(9, d_rows(r), dinv_r).start()
        go(d_rows(2 * x + 1 - c), dinv_r, ("dinv",), ("dinv",), sib)

    at_home(home_start)
    local(4, dinv, dinv_v).start()
    local(5, dqd, own_v).start()
    az_near()

    def home_1():
        ay_send(1)
        for i in first:
            x_forward(i)

    def own_from_away(i):
        sw_got(PANEL, i)
        x_own(i)

    def away_1():
        ay_send(0)
        az_far()
        pl.semaphore_signal(ready, inc=1, device_id=partner, device_id_type=MESH)
        ay_send(1)
        pl.semaphore_wait(ready, 1)
        for i in range(nk):
            sw_send(PANEL, i)
        for i in range(ns):
            sw_send(DQ, i)
        for i in first:
            own_from_away(i)

    at_home(home_1)
    at_away(away_1)
    ay_forward(0)

    def home_2():
        for i in middle:
            x_forward(i)
        for i in last:
            own_from_home(i)
        for i in first:
            x_far(i)

    def away_2():
        for i in middle:
            own_from_away(i)
        for i in first:
            x_forward(i)

    at_home(home_2)
    at_away(away_2)
    ay_forward(1)

    def home_3():
        for i in middle:
            x_far(i)
        turn_own()
        local(1, dq, dqv).wait()
        local(2, dqd, dqd_v).wait()
        local(9, d_rows(r), dinv_r).wait()
        for i in last:
            x_forward(i)
        for i in last:
            x_far(i)

    def away_3():
        for i in last:
            own_from_away(i)
        turn_own()
        for i in middle:
            x_forward(i)
        got(dqd_v, "dqd")
        got(dinv_r, "dinv")
        got(st_v, "st")
        for i in first:
            x_far(i)
        sw_got(DQ, 0)

    at_home(home_3)
    at_away(away_3)
    own_trace()
    cp = local(3, st_v, st_s)
    cp.start()
    cp.wait()
    trs[...] = jnp.zeros_like(trs)
    ay_done()
    ahead = list(last)
    for i in first:
        x_sib(i)
        compute(i)
        if ahead:
            at_away(lambda: x_forward(ahead[0]))
            ahead.pop(0)
    for i in ahead:
        at_away(lambda i=i: x_forward(i))
    for i in first:
        rs_a(i)

    def away_4():
        for i in range(1, ns - 1):
            sw_got(DQ, i)

    at_away(away_4)
    for i in middle:
        at_away(lambda i=i: x_far(i))
        x_sib(i)
        compute(i)
    def home_5():
        for i in middle:
            rs_a(i)

    def away_5():
        x_far(last[0])
        sw_got(DQ, ns - 1)

    at_home(home_5)
    at_away(away_5)
    x_sib(last[0])
    compute(last[0])

    def away_6():
        for i in last[1:]:
            x_far(i)
        for i in first:
            rs_b(i)
        for i in middle:
            rs_a(i)

    at_away(away_6)
    for i in last[1:]:
        x_sib(i)
        compute(i)
    trace_send()

    for i in last:
        rs_a(i)

    def away_7():
        for i in middle:
            rs_b(i)
        for i in first:
            rs_c(i)

    at_away(away_7)

    def home_turn():
        trace_sum()
        pl.semaphore_wait(turn, 1)
        for i in first:
            rs_b(i)

    at_home(home_turn)
    for i in last:
        rs_b(i)
    at_away(lambda: pl.semaphore_signal(turn, inc=1, device_id=sib, device_id_type=MESH))

    def home_7():
        for i in middle:
            rs_b(i)
        for i in first:
            rs_c(i)

    at_home(home_7)
    for i in middle:
        rs_c(i)
    for i in last:
        rs_c(i)

    def home_end():
        for i in range(nk):
            s, off, wc = chunks[i]
            local(10 + i, cbuf.at[cols(i)], out_panel.at[cols(i)]).wait()
            part = pl.ds(off, wc)
            local(26 + i, fsrc.at[s, :, part], out_sum.at[s, :, part]).wait()
        gone(st_v, "st")
        gone(dqd, "dqd")
        gone(dinv_r, "dinv")
        gone(tsum, "small")

    def away_end():
        gone(own_piece, "piece")
        gone(panel, "panel")
        gone(dq, "dq")
        gone(cbuf, "selected")
        gone(fsrc, "sums")
        gone(trs, "tile")
        got(out_panel, "selected")
        got(out_sum, "sums")

    gone(sig.at[pl.ds(0, 15)], "pieces")
    for i in range(nk):
        s, off, wc = chunks[i]
        gone(bs[i].at[pl.ds(0, 7)], "x", i)
        gone(ip.at[s, pl.ds(0, 7), :, pl.ds(off, wc)], "rs", i)
    gone(tra.at[pl.ds(0, 3)], "tiles")
    at_home(home_end)
    at_away(away_end)
    trace_got()


def write_kernel(p_in, diag_in, tr_in, p_out, diag_out, tr_out, tv, sem):
    ns = p_in.shape[0]
    copies = [
        pltpu.make_async_copy(src, dst, sem.at[i])
        for i, (src, dst) in enumerate(((tr_in, tv), (p_in, p_out), (diag_in, diag_out)))
    ]
    for copy in copies:
        copy.start()
    copies[0].wait()
    total = tv[0] + tv[1]
    for i in range(ns):
        tr_out[i] = jnp.sum(total[i : i + 1, :1])
    copies[1].wait()
    copies[2].wait()


def local(sigma_anc, panel, structure, d_inv, dq_panel, dq_diag):
    ns, w = panel.shape[0], panel.shape[2]
    share = w // 8
    chunks = chunks_of(ns, w)
    n_send, n_recv = all_slots(ns, len(chunks))[2:]
    bf, f32 = jnp.bfloat16, jnp.float32
    anywhere = pl.BlockSpec(memory_space=pl.ANY)
    hbm = pl.BlockSpec(memory_space=pltpu.HBM)
    smem = pl.BlockSpec(memory_space=pltpu.SMEM)
    found, sums, tr = pl.pallas_call(
        functools.partial(kernel, chunks),
        out_shape=(
            jax.ShapeDtypeStruct((ns, w, w), bf),
            jax.ShapeDtypeStruct((ns, share, w), f32),
            jax.ShapeDtypeStruct((2, 8, 128), f32),
        ),
        in_specs=[hbm] * 6,
        out_specs=(anywhere, anywhere, anywhere),
        scratch_shapes=[
            pltpu.VMEM((16, w, w // 2), bf),
            *[pltpu.VMEM((8, w, wc), bf) for _, _, wc in chunks],
            pltpu.VMEM((w, w), f32),
            pltpu.VMEM((ns, w, w), bf),
            pltpu.VMEM((ns, w, w), bf),
            pltpu.VMEM((ns, w, w), bf),
            pltpu.VMEM((ns, 8, share, w), f32),
            pltpu.VMEM((ns, 4, share, w), f32),
            pltpu.VMEM((ns, 4, share, w), f32),
            pltpu.VMEM((ns, 2, share // 2, w), f32),
            pltpu.VMEM((ns, 2, share, w), f32),
            pltpu.VMEM((ns, share, w), f32),
            pltpu.VMEM((ns, w, w), bf),
            pltpu.VMEM((ns, w, w), bf),
            pltpu.VMEM((ns, share, w), bf),
            pltpu.VMEM((ns, w, w), bf),
            pltpu.VMEM((8, 128), f32),
            pltpu.VMEM((8, 128), f32),
            pltpu.VMEM((8, 8, 128), f32),
            pltpu.VMEM((8, 128), f32),
            pltpu.VMEM((8, 128), jnp.int32),
            pltpu.SMEM((8, 128), jnp.int32),
            pltpu.SMEM(structure.shape, jnp.int32),
            pltpu.SemaphoreType.DMA((n_send,)),
            pltpu.SemaphoreType.DMA((n_recv,)),
            pltpu.SemaphoreType.DMA((32,)),
            pltpu.SemaphoreType.REGULAR,
            pltpu.SemaphoreType.REGULAR,
        ],
        compiler_params=pltpu.CompilerParams(
            collective_id=0, has_side_effects=True, vmem_limit_bytes=44 * 1024 * 1024
        ),
        name="selected_inverse",
    )(*(pltpu.with_memory_space_constraint(v, pltpu.HBM) for v in (structure, sigma_anc, panel, dq_panel, dq_diag, d_inv)))
    return pl.pallas_call(
        write_kernel,
        out_shape=(
            jax.ShapeDtypeStruct((ns, w, w), bf),
            jax.ShapeDtypeStruct((ns, share, w), f32),
            jax.ShapeDtypeStruct((ns,), f32),
        ),
        in_specs=[anywhere] * 3,
        out_specs=(hbm, hbm, smem),
        scratch_shapes=[
            pltpu.VMEM((2, 8, 128), f32),
            pltpu.SemaphoreType.DMA((3,)),
        ],
        compiler_params=pltpu.CompilerParams(vmem_limit_bytes=4 * 1024 * 1024),
        name="write_results",
    )(found, sums, tr)


def solution(mesh):
    return jax.shard_map(
        local,
        mesh=mesh,
        in_specs=(
            P("row", "col"),
            P("col", "row", None),
            P("col", None),
            P("col", None, None),
            P("col", "row", None),
            P("col", None, None),
        ),
        out_specs=(P("col", "row", None), P("col", "row", None), P("col")),
        check_vma=False,
    )
```

```python
import functools

import jax
import jax.numpy as jnp
from jax import lax
from jax.experimental import pallas as pl
from jax.experimental.pallas import tpu as pltpu
from jax.sharding import PartitionSpec as P

MESH = pl.DeviceIdType.MESH
PANEL, DQ, SEL = 0, 1, 2
SPLIT = (2, 2, 2)


def chunks_of(ns, w):
    out = []
    for i in range(ns):
        n = SPLIT[i % len(SPLIT)]
        out += [(i, j * (w // n), w // n) for j in range(n)]
    return out


class Slots:
    def __init__(self):
        self.at = {}

    def __call__(self, *name, span=1):
        if name not in self.at:
            self.at[name] = sum(self.size.values()) if hasattr(self, "size") else 0
            self.size = getattr(self, "size", {})
            self.size[name] = span
        return self.at[name]


def all_slots(ns, nk):
    send, recv = Slots(), Slots()
    for name in ("pieces", "piece", "panel", "dq", "selected", "sums", "tiles", "tile", "small", "st", "dqd", "dinv"):
        send(name)
    for i in range(nk):
        send("x", i)
        send("rs", i)
    for name in ("st", "dqd", "dinv", "az_own", "az_nb", "az_nb2", "az_far", "ayf", "selected", "sums", "tiles", "trz"):
        recv(name)
    for j in range(2):
        recv("ay", j)
    for i in range(nk):
        for name in ("xo", "xf", "xs", "rs1", "rsa", "rsb", "panel"):
            recv(name, i)
    for i in range(ns):
        recv("dq", i)
    return send, recv, sum(send.size.values()), sum(recv.size.values())


def kernel(
    chunks, struct, sigma, panel, dq, dqd, dinv,
    out_panel, out_sum, out_tr,
    sig, *rest,
):
    nk = len(chunks)
    ns = chunks[-1][0] + 1
    bs = rest[:nk]
    (dqv, cbuf, own_t, ip, rk, sx, ra, rr, fsrc, dqd_v, dinv_v, dinv_r, own_v, td, trs, tra, tsum, st_v, st_s, st_in,
     send_sem, recv_sem, loc_sem, ready, turn) = rest[nk + 1 :]
    prod = rest[nk]
    w = dqv.shape[1]
    hw = w // 2
    share = w // 8
    send_at, recv_at = all_slots(ns, nk)[:2]

    row, col = lax.axis_index("row"), lax.axis_index("col")
    x, zh = row // 2, row % 2
    y, zl, c = col // 4, (col // 2) % 2, col % 2
    z = zh * 2 + zl
    home = c == zh
    hb = 1 - (c + zh) % 2
    up = (hb + zl) % 2
    r = 2 * x + c
    xp, xm, xq = (x + 1) % 4, (x + 3) % 4, (x + 2) % 4
    yp, ym, yq = (y + 1) % 4, (y + 3) % 4, (y + 2) % 4
    zp, zm, zq = (z + 1) % 4, (z + 3) % 4, (z + 2) % 4

    def dev(x_, y_, z_, c_):
        return (x_ * 2 + z_ // 2, (y_ * 2 + z_ % 2) * 2 + c_)

    sib = dev(x, y, z, 1 - c)
    partner = dev(x, y, zq, 1 - c)


    def go(src, dst, sname, rname, to):
        pltpu.make_async_remote_copy(
            src_ref=src,
            dst_ref=dst,
            send_sem=send_sem.at[send_at(*sname)],
            recv_sem=recv_sem.at[recv_at(*rname)],
            device_id=to,
            device_id_type=MESH,
        ).start()

    def got(dst, *name):
        pltpu.make_async_copy(dst, dst, recv_sem.at[recv_at(*name)]).wait()

    def gone(src, *name):
        pltpu.make_async_copy(src, src, send_sem.at[send_at(*name)]).wait()

    def local(i, src, dst):
        return pltpu.make_async_copy(src, dst, loc_sem.at[i])

    def at_home(f):
        pl.when(home)(f)

    def at_away(f):
        pl.when(jnp.logical_not(home))(f)

    own_piece = sig.at[4 * y + 2 * zl + c]

    def az_send():
        for d in range(2):
            for z_, h in ((zp, d), (zm, 1 - d)):
                rows = pl.ds(h * hw, hw)
                go(sigma.at[rows], sig.at[4 * y + 2 * zl + c, rows], ("pieces",), (("az_nb", "az_nb2")[d],),
                   dev(x, y, z_, zh))

    def az_own_away():
        go(sigma, own_piece, ("piece",), ("az_own",), sib)

    def az_near():
        part = sig.at[pl.ds(4 * y + 2 * (1 - zl), 2), pl.ds(pl.multiple_of(up * hw, hw), hw)]
        got(part, "az_nb")
        go(part, part, ("pieces",), ("az_far",), dev(x, y, (z + 1 + 2 * up) % 4, c))
        got(part, "az_nb2")

    def az_far():
        got(sig.at[pl.ds(4 * y + 2 * zl, 2)], "az_far")

    pair_zl = ((zl * hb + (1 - zl) * (1 - hb)), ((1 - zl) * hb + zl * (1 - hb)))

    def pair(y_, j):
        return sig.at[pl.ds(4 * y_ + 2 * pair_zl[j], 2)]

    def ay_send(j):
        go(pair(y, j), pair(y, j), ("pieces",), ("ay", j), dev(x, yp, z, c))
        go(pair(y, j), pair(y, j), ("pieces",), ("ay", j), dev(x, ym, z, c))

    def ay_forward(j):
        got(sig.at[pl.ds(0, 4)], "ay", j)
        p0 = sig.at[4 * ym + 2 * pair_zl[j]]
        go(p0, p0, ("pieces",), ("ayf",), dev(x, yp, z, c))
        p1 = sig.at[4 * yp + 2 * pair_zl[j] + 1]
        go(p1, p1, ("pieces",), ("ayf",), dev(x, ym, z, c))

    def ay_done():
        got(sig.at[pl.ds(4 * yq, 4)], "ayf")

    def blk(i, x_, c_=None):
        return bs[i].at[2 * x_ + (c if c_ is None else c_)]

    def half(i, x_, d):
        return bs[i].at[2 * x_ + c, pl.ds(d * hw, hw)]

    def to_sib(i, x_):
        go(blk(i, x_), blk(i, x_), ("x", i), ("xs", i), sib)

    def x_own(i):
        go(blk(i, x), blk(i, x), ("x", i), ("xo", i), dev(xp, y, z, c))
        go(blk(i, x), blk(i, x), ("x", i), ("xo", i), dev(xm, y, z, c))
        to_sib(i, x)

    def x_forward(i):
        got(bs[i].at[pl.ds(0, 2)], "xo", i)
        go(half(i, xm, 0), half(i, xm, 0), ("x", i), ("xf", i), dev(xp, y, z, c))
        go(half(i, xp, 1), half(i, xp, 1), ("x", i), ("xf", i), dev(xm, y, z, c))
        to_sib(i, xm)
        to_sib(i, xp)

    def x_far(i):
        got(blk(i, xq), "xf", i)
        to_sib(i, xq)

    def x_sib(i):
        got(bs[i].at[pl.ds(0, 4)], "xs", i)

    def cols(i):
        return chunks[i][0], slice(None), pl.ds(chunks[i][1], chunks[i][2])

    def sw_dst(kind, i, r_):
        if kind == PANEL:
            return bs[i].at[r_]
        return dqv.at[i] if kind == DQ else out_panel.at[cols(i)]

    def sw_send(kind, i):
        src = panel.at[cols(i)] if kind == PANEL else dq.at[i] if kind == DQ else cbuf.at[cols(i)]
        name = ("panel", "dq", "selected")[kind]
        go(src, sw_dst(kind, i, 2 * x + 1 - c), (name,), (name,) if kind == SEL else (name, i), partner)

    def sw_got(kind, i):
        got(sw_dst(kind, i, r), ("panel", "dq")[kind], i)

    def turn_own():
        for i, (s, off, wc) in enumerate(chunks):
            own_t[s, off : off + wc, :] = bs[i][r].T

    def compute(i):
        b = bs[i]
        s, off, wc = chunks[i]
        lanes = slice(off, off + wc)

        def step(t, carry):
            k = st_s[s, t]
            v = jnp.dot(sig[2 * k], b[k, :hw], preferred_element_type=jnp.float32)
            v += jnp.dot(sig[2 * k + 1], b[k, hw:], preferred_element_type=jnp.float32)
            prod[:, :wc] += v
            return carry

        prod[:, :wc] = jnp.zeros((w, wc), jnp.float32)
        lax.fori_loop(0, 4, step, 0)
        here = jnp.float32(0)
        for t in range(4):
            here += jnp.where(st_s[s, t] == r, jnp.float32(1), jnp.float32(0))
        kept = prod[:, :wc] * here
        hi = kept.astype(jnp.bfloat16)
        cbuf[s, :, lanes] = -hi

        def selected_home():
            local(10 + i, cbuf.at[cols(i)], out_panel.at[cols(i)]).start()

        at_home(selected_home)
        at_away(lambda: sw_send(SEL, i))
        lo = (kept - hi.astype(jnp.float32)).astype(jnp.bfloat16)
        trace = -2.0 * jnp.sum(kept * dqv[s, :, lanes].astype(jnp.float32), axis=0, keepdims=True)
        inner = jnp.dot(own_t[s], hi, preferred_element_type=jnp.float32)
        inner += jnp.dot(own_t[s], lo, preferred_element_type=jnp.float32)
        for a in range(8):
            ip[s, 4 * (a % 2) + a // 2, :, lanes] = inner[a * share : (a + 1) * share]
        trace += jnp.sum(inner * dqd_v[s, :, lanes].astype(jnp.float32), axis=0, keepdims=True)
        part = pl.ds(off, wc)
        go(ip.at[s, pl.ds(4 * (1 - c), 4), :, part], rk.at[s, :, :, part], ("rs", i), ("rs1", i), sib)
        trs[s : s + 1, :] += jnp.broadcast_to(jnp.sum(trace, axis=1, keepdims=True), (1, 128))

    hs = share // 2
    near = (xp, xm)

    def rs_a(i):
        s, off, wc = chunks[i]
        lanes, part = slice(off, off + wc), pl.ds(off, wc)
        got(rk.at[s, :, :, part], "rs1", i)
        sx[s, :, :, lanes] = ip[s, pl.ds(4 * c, 4), :, lanes] + rk[s, :, :, lanes]
        for d in range(2):
            go(sx.at[s, xq, pl.ds(d * hs, hs), part], ra.at[s, d, :, part], ("rs", i), ("rsa", i),
               dev(near[d], y, z, c))

    def rs_b(i):
        s, off, wc = chunks[i]
        lanes, part = slice(off, off + wc), pl.ds(off, wc)
        got(ra.at[s, :, :, part], "rsa", i)
        for d in range(2):
            sx[s, near[d], d * hs : (d + 1) * hs, lanes] += ra[s, d, :, lanes]
            go(sx.at[s, near[d], :, part], rr.at[s, d, :, part], ("rs", i), ("rsb", i), dev(near[d], y, z, c))

    def rs_c(i):
        s, off, wc = chunks[i]
        lanes, part = slice(off, off + wc), pl.ds(off, wc)
        got(rr.at[s, :, :, part], "rsb", i)
        total = sx[s, x, :, lanes] + rr[s, 0, :, lanes] + rr[s, 1, :, lanes]
        fsrc[s, :, lanes] = dinv_r[s, :, lanes].astype(jnp.float32) + total

        at_home(lambda: local(26 + i, fsrc.at[s, :, part], out_sum.at[s, :, part]).start())
        at_away(lambda: go(fsrc.at[s, :, part], out_sum.at[s, :, part], ("sums",), ("sums",), partner))

    def own_trace():
        local(4, dinv, dinv_v).wait()
        local(5, dqd, own_v).wait()
        td[...] = jnp.zeros_like(td)
        for i in range(ns):
            v = jnp.sum(dinv_v[i].astype(jnp.float32) * own_v[i].astype(jnp.float32), axis=0, keepdims=True)
            td[i : i + 1, :] = jnp.broadcast_to(jnp.sum(v, axis=1, keepdims=True), (1, 128))
        local(6, td, out_tr.at[1]).start()

    def trace_send():
        def tile(dx, name):
            go(trs, tra.at[2 * dx + c], (name,), ("tiles",), dev((x + dx) % 4, y, z, zh))

        at_away(lambda: tile(0, "tile"))
        at_home(keep_tile)
        for dx in range(1, 4):
            tile(dx, "tiles")

    def keep_tile():
        tsum[...] = trs[...]

    def trace_sum():
        got(tra.at[pl.ds(0, 7)], "tiles")
        total = tsum[...]
        for k in range(2, 8):
            total += tra[k]
        tsum[...] = total + tra[1 - c]
        local(8, tsum, out_tr.at[0]).start()
        go(tsum, out_tr.at[0], ("small",), ("trz",), dev(x, y, zq, c))

    def trace_got():
        local(6, td, out_tr.at[1]).wait()
        at_home(lambda: local(8, tsum, out_tr.at[0]).wait())
        at_away(lambda: got(out_tr.at[0], "trz"))

    barrier = pltpu.get_barrier_semaphore()
    peers = [dev(x, yp, z, c), dev(x, ym, z, c), sib]
    for c_ in (0, 1):
        peers += [dev(x_, y, z, c_) for x_ in (xp, xm, xq)]
        peers += [dev(x, y, z_, c_) for z_ in (zp, zm, zq)]
    for peer in peers:
        pl.semaphore_signal(barrier, inc=1, device_id=peer, device_id_type=MESH)

    at_home(lambda: [local(20 + i, panel.at[cols(i)], bs[i].at[r]).start() for i in range(nk)] and None)
    at_home(lambda: local(0, sigma, own_piece).start())
    at_home(lambda: local(7, struct, st_in).start())

    def structure_out():
        rows = lax.broadcasted_iota(jnp.int32, st_v.shape, 0)
        lanes = lax.broadcasted_iota(jnp.int32, st_v.shape, 1)
        local(7, struct, st_in).wait()
        v = jnp.zeros(st_v.shape, jnp.int32)
        for i in range(ns):
            for t in range(4):
                v = jnp.where((rows == i) & (lanes == t), st_in[i, t], v)
        st_v[...] = v

    at_home(structure_out)
    pl.semaphore_wait(barrier, len(peers))

    az_send()
    at_away(az_own_away)
    at_home(lambda: go(st_v, st_v, ("st",), ("st",), sib))
    last = [i for i in range(nk) if chunks[i][0] == ns - 1]
    early = [i for i in range(nk) if i not in last]
    first = [i for i in early if chunks[i][0] == 0]
    middle = [i for i in early if i not in first]

    def own_from_home(i):
        local(20 + i, panel.at[cols(i)], bs[i].at[r]).wait()
        x_own(i)

    def d_rows(r_):
        return dinv.at[:, pl.ds(pl.multiple_of(r_ * share, share), share)]

    def home_start():
        for i in early:
            own_from_home(i)
        local(0, sigma, own_piece).wait()
        got(own_piece, "az_own")
        ay_send(0)
        local(1, dq, dqv).start()
        local(2, dqd, dqd_v).start()
        go(dqd, dqd_v, ("dqd",), ("dqd",), sib)
        local(9, d_rows(r), dinv_r).start()
        go(d_rows(2 * x + 1 - c), dinv_r, ("dinv",), ("dinv",), sib)

    at_home(home_start)
    local(4, dinv, dinv_v).start()
    local(5, dqd, own_v).start()
    az_near()

    def home_1():
        ay_send(1)
        for i in first:
            x_forward(i)

    def own_from_away(i):
        sw_got(PANEL, i)
        x_own(i)

    def away_1():
        ay_send(0)
        az_far()
        pl.semaphore_signal(ready, inc=1, device_id=partner, device_id_type=MESH)
        ay_send(1)
        pl.semaphore_wait(ready, 1)
        for i in range(nk):
            sw_send(PANEL, i)
        for i in range(ns):
            sw_send(DQ, i)
        for i in first:
            own_from_away(i)

    at_home(home_1)
    at_away(away_1)
    ay_forward(0)

    def home_2():
        for i in middle:
            x_forward(i)
        for i in last:
            own_from_home(i)
        for i in first:
            x_far(i)

    def away_2():
        for i in middle:
            own_from_away(i)
        for i in first:
            x_forward(i)

    at_home(home_2)
    at_away(away_2)
    ay_forward(1)

    def home_3():
        for i in middle:
            x_far(i)
        turn_own()
        local(1, dq, dqv).wait()
        local(2, dqd, dqd_v).wait()
        local(9, d_rows(r), dinv_r).wait()
        for i in last:
            x_forward(i)
        for i in last:
            x_far(i)

    def away_3():
        for i in last:
            own_from_away(i)
        turn_own()
        for i in middle:
            x_forward(i)
        got(dqd_v, "dqd")
        got(dinv_r, "dinv")
        got(st_v, "st")
        for i in first:
            x_far(i)
        sw_got(DQ, 0)

    at_home(home_3)
    at_away(away_3)
    own_trace()
    cp = local(3, st_v, st_s)
    cp.start()
    cp.wait()
    trs[...] = jnp.zeros_like(trs)
    ay_done()
    ahead = list(last)
    for i in first:
        x_sib(i)
        compute(i)
        if ahead:
            at_away(lambda: x_forward(ahead[0]))
            ahead.pop(0)
    for i in ahead:
        at_away(lambda i=i: x_forward(i))
    for i in first:
        rs_a(i)

    def away_4():
        for i in range(1, ns - 1):
            sw_got(DQ, i)

    at_away(away_4)
    for i in middle:
        at_away(lambda i=i: x_far(i))
        x_sib(i)
        compute(i)
    def home_5():
        for i in middle:
            rs_a(i)

    def away_5():
        x_far(last[0])
        for i in first:
            rs_b(i)
        for i in last[1:]:
            x_far(i)
        sw_got(DQ, ns - 1)

    at_home(home_5)
    at_away(away_5)
    x_sib(last[0])
    compute(last[0])

    def away_6():
        for i in middle:
            rs_a(i)

    at_away(away_6)
    for i in last[1:]:
        x_sib(i)
        compute(i)
    trace_send()

    for i in last:
        rs_a(i)

    def away_7():
        for i in middle:
            rs_b(i)
        for i in first:
            rs_c(i)

    at_away(away_7)

    def home_turn():
        trace_sum()
        pl.semaphore_wait(turn, 1)
        for i in first:
            rs_b(i)

    at_home(home_turn)
    for i in last:
        rs_b(i)
    at_away(lambda: pl.semaphore_signal(turn, inc=1, device_id=sib, device_id_type=MESH))

    def home_7():
        for i in middle:
            rs_b(i)
        for i in first:
            rs_c(i)

    at_home(home_7)
    for i in middle:
        rs_c(i)
    for i in last:
        rs_c(i)

    def home_end():
        for i in range(nk):
            s, off, wc = chunks[i]
            local(10 + i, cbuf.at[cols(i)], out_panel.at[cols(i)]).wait()
            part = pl.ds(off, wc)
            local(26 + i, fsrc.at[s, :, part], out_sum.at[s, :, part]).wait()
        gone(st_v, "st")
        gone(dqd, "dqd")
        gone(dinv_r, "dinv")
        gone(tsum, "small")

    def away_end():
        gone(own_piece, "piece")
        gone(panel, "panel")
        gone(dq, "dq")
        gone(cbuf, "selected")
        gone(fsrc, "sums")
        gone(trs, "tile")
        got(out_panel, "selected")
        got(out_sum, "sums")

    gone(sig.at[pl.ds(0, 15)], "pieces")
    for i in range(nk):
        s, off, wc = chunks[i]
        gone(bs[i].at[pl.ds(0, 7)], "x", i)
        gone(ip.at[s, pl.ds(0, 7), :, pl.ds(off, wc)], "rs", i)
    gone(tra.at[pl.ds(0, 3)], "tiles")
    at_home(home_end)
    at_away(away_end)
    trace_got()


def write_kernel(p_in, diag_in, tr_in, p_out, diag_out, tr_out, tv, sem):
    ns = p_in.shape[0]
    copies = [
        pltpu.make_async_copy(src, dst, sem.at[i])
        for i, (src, dst) in enumerate(((tr_in, tv), (p_in, p_out), (diag_in, diag_out)))
    ]
    for copy in copies:
        copy.start()
    copies[0].wait()
    total = tv[0] + tv[1]
    for i in range(ns):
        tr_out[i] = jnp.sum(total[i : i + 1, :1])
    copies[1].wait()
    copies[2].wait()


def local(sigma_anc, panel, structure, d_inv, dq_panel, dq_diag):
    ns, w = panel.shape[0], panel.shape[2]
    share = w // 8
    chunks = chunks_of(ns, w)
    n_send, n_recv = all_slots(ns, len(chunks))[2:]
    bf, f32 = jnp.bfloat16, jnp.float32
    anywhere = pl.BlockSpec(memory_space=pl.ANY)
    hbm = pl.BlockSpec(memory_space=pltpu.HBM)
    smem = pl.BlockSpec(memory_space=pltpu.SMEM)
    found, sums, tr = pl.pallas_call(
        functools.partial(kernel, chunks),
        out_shape=(
            jax.ShapeDtypeStruct((ns, w, w), bf),
            jax.ShapeDtypeStruct((ns, share, w), f32),
            jax.ShapeDtypeStruct((2, 8, 128), f32),
        ),
        in_specs=[hbm] * 6,
        out_specs=(anywhere, anywhere, anywhere),
        scratch_shapes=[
            pltpu.VMEM((16, w, w // 2), bf),
            *[pltpu.VMEM((8, w, wc), bf) for _, _, wc in chunks],
            pltpu.VMEM((w, w), f32),
            pltpu.VMEM((ns, w, w), bf),
            pltpu.VMEM((ns, w, w), bf),
            pltpu.VMEM((ns, w, w), bf),
            pltpu.VMEM((ns, 8, share, w), f32),
            pltpu.VMEM((ns, 4, share, w), f32),
            pltpu.VMEM((ns, 4, share, w), f32),
            pltpu.VMEM((ns, 2, share // 2, w), f32),
            pltpu.VMEM((ns, 2, share, w), f32),
            pltpu.VMEM((ns, share, w), f32),
            pltpu.VMEM((ns, w, w), bf),
            pltpu.VMEM((ns, w, w), bf),
            pltpu.VMEM((ns, share, w), bf),
            pltpu.VMEM((ns, w, w), bf),
            pltpu.VMEM((8, 128), f32),
            pltpu.VMEM((8, 128), f32),
            pltpu.VMEM((8, 8, 128), f32),
            pltpu.VMEM((8, 128), f32),
            pltpu.VMEM((8, 128), jnp.int32),
            pltpu.SMEM((8, 128), jnp.int32),
            pltpu.SMEM(structure.shape, jnp.int32),
            pltpu.SemaphoreType.DMA((n_send,)),
            pltpu.SemaphoreType.DMA((n_recv,)),
            pltpu.SemaphoreType.DMA((32,)),
            pltpu.SemaphoreType.REGULAR,
            pltpu.SemaphoreType.REGULAR,
        ],
        compiler_params=pltpu.CompilerParams(
            collective_id=0, has_side_effects=True, vmem_limit_bytes=44 * 1024 * 1024
        ),
        name="selected_inverse",
    )(*(pltpu.with_memory_space_constraint(v, pltpu.HBM) for v in (structure, sigma_anc, panel, dq_panel, dq_diag, d_inv)))
    return pl.pallas_call(
        write_kernel,
        out_shape=(
            jax.ShapeDtypeStruct((ns, w, w), bf),
            jax.ShapeDtypeStruct((ns, share, w), f32),
            jax.ShapeDtypeStruct((ns,), f32),
        ),
        in_specs=[anywhere] * 3,
        out_specs=(hbm, hbm, smem),
        scratch_shapes=[
            pltpu.VMEM((2, 8, 128), f32),
            pltpu.SemaphoreType.DMA((3,)),
        ],
        compiler_params=pltpu.CompilerParams(vmem_limit_bytes=4 * 1024 * 1024),
        name="write_results",
    )(found, sums, tr)


def solution(mesh):
    return jax.shard_map(
        local,
        mesh=mesh,
        in_specs=(
            P("row", "col"),
            P("col", "row", None),
            P("col", None),
            P("col", None, None),
            P("col", "row", None),
            P("col", None, None),
        ),
        out_specs=(P("col", "row", None), P("col", "row", None), P("col")),
        check_vma=False,
    )
```
